32 devices in a mesh: tm: 8 (over z, x), rows: 4 (over y, core).
Axes of the slice: x: 2, y: 2, z: 4, core: 2. Of those that a mesh axis runs over, the one named last changes fastest.
Arguments:
- frames: bfloat16 [8, 32, 64, 128], P('tm', 'rows'), may hold values from -6 to 6
- decays: float32 [8, 256], P('tm'), may hold values from 0.4 to 1
- in_weight: bfloat16 [3, 3, 128, 256], replicated, may hold values from -0.046875 to 0.046875
- out_weight: bfloat16 [3, 3, 256, 128], replicated, may hold values from -0.125 to 0.125
- skip_gain: float32 [128], replicated, may hold values from 0.25 to 1.75
- cotangent: bfloat16 [8, 32, 64, 128], P('tm', 'rows'), may hold values from -6 to 6
Outputs:
- output_frames: bfloat16 [8, 32, 64, 128], P('tm', 'rows')
- input_grad: bfloat16 [8, 32, 64, 128], P('tm', 'rows')
- in_weight_grad: float32 [3, 3, 128, 256], replicated
- out_weight_grad: float32 [3, 3, 256, 128], replicated
- gain_grad: float32 [128], replicated
- decay_grad: float32 [8, 256], P('tm')
The draws below stay inside these ranges and needn't reach their ends.
All inputs are finite; a program needn't handle non-finite values.
Results may differ from the reference program's by a relative error of at most 0.008.
Values may be sent and summed in bfloat16 or wider, within the bound.
A program may use at most 192 MiB of HBM per device.

```python
import math
import jax
import jax.numpy as jnp
from jax import lax

CH = 128
S = 256
H = 32
W = 64
FRAMES = 8


def draw_decays(key, part):
    keys = jax.random.split(key, 6)
    fast_share = 0.5
    fast_mask = jax.random.uniform(keys[0], (S,), jnp.float32) < fast_share
    slow_rate = jax.random.uniform(keys[1], (S,), jnp.float32, 0.05, 0.5) * 2.3 / FRAMES
    fast_rate = jax.random.uniform(keys[2], (S,), jnp.float32, 1.0 / 50.0, 1.0 / 30.0)
    baseline_rate = jnp.where(fast_mask, fast_rate, slow_rate)
    random_wobble = jnp.exp(jax.random.uniform(keys[3], (FRAMES, S), jnp.float32, -0.7, 0.7))
    marked_places = jax.random.randint(keys[4], (3,), 0, FRAMES)
    position_list = jnp.arange(FRAMES)
    sudden_spike = jnp.any(position_list[:, None] == marked_places[None, :], axis=1)
    multiplier = jax.random.uniform(keys[5], (FRAMES, S), jnp.float32, 0.6, 0.8)
    decay_factor = jnp.exp(-baseline_rate[None, :] * random_wobble) * jnp.where(sudden_spike[:, None], multiplier, 1.0)
    return decay_factor.astype(jnp.float32)


def levels(key, extent, cuts, least, top_value):
    def one(dim, shards_of):
        steps = jax.random.uniform(jax.random.fold_in(jax.random.fold_in(key, 6), dim), (shards_of,), jnp.float32, least / len(cuts), top_value / len(cuts))
        return jnp.repeat(jnp.exp(steps), extent[dim] // shards_of).reshape((-1,) + (1,) * (len(extent) - dim - 1))

    level = one(*cuts[0])
    for cut in cuts[1:]:
        level = level * one(*cut)
    return level


def noise(rng, extent, spread, most, cuts=(), kind=jnp.bfloat16):
    factor_of = levels(rng, extent, cuts, -0.22, 0.18) if cuts else 1.0
    array = jax.random.normal(rng, extent, jnp.float32) * spread * factor_of
    return jnp.minimum(jnp.maximum(array, -most), most).astype(kind)


def setup_inputs(seed: int = 0) -> dict:
    seeds = jax.random.split(jax.random.key(seed), 7)
    return {
        "frames": noise(seeds[0], (FRAMES, H, W, CH), 1.0, 6.0, ((0, 8), (1, 4))),
        "decays": draw_decays(jax.random.fold_in(seeds[6], 71), 0),
        "in_weight": noise(seeds[2], (3, 3, CH, S), (144 * CH) ** -0.5, 0.046875),
        "out_weight": noise(seeds[3], (3, 3, S, CH), (9 * S) ** -0.5, 0.125),
        "skip_gain": jnp.clip(1.0 + 0.15 * jax.random.normal(seeds[4], (CH,), jnp.float32), 0.25, 1.75),
        "cotangent": noise(seeds[5], (FRAMES, H, W, CH), 1.0, 6.0, ((0, 8), (1, 4))),
    }


def pad_frames(field):
    return jnp.pad(field, ((0, 0), (1, 1), (1, 1), (0, 0)))

def conv_taps(padded, weights):
    frame_count = padded.shape[0]
    height = padded.shape[1] - 2
    across = padded.shape[2] - 2
    channels = padded.shape[3]
    result = jnp.zeros((frame_count * height * across, weights.shape[3]), jnp.float32)
    for row_tap in range(3):
        for col_tap in range(3):
            window = padded[:, row_tap:row_tap + height, col_tap:col_tap + across, :].reshape(-1, channels)
            result = result + jnp.dot(window, weights[row_tap, col_tap], preferred_element_type=jnp.float32)
    return result.reshape(frame_count, height, across, weights.shape[3])

def tap_grads(padded, grad_field):
    height = grad_field.shape[1]
    across = grad_field.shape[2]
    channels = padded.shape[3]
    flat_grad = grad_field.reshape(-1, grad_field.shape[3])
    outer_list = []
    for row_tap in range(3):
        inner_list = []
        for col_tap in range(3):
            window = padded[:, row_tap:row_tap + height, col_tap:col_tap + across, :].reshape(-1, channels)
            inner_list.append(lax.dot_general(window, flat_grad, (((0,), (0,)), ((), ())), preferred_element_type=jnp.float32))
        outer_list.append(jnp.stack(inner_list))
    return jnp.stack(outer_list)

def flipped(weights):
    return jnp.transpose(weights[::-1, ::-1], (0, 1, 3, 2))

def reference(frames, decays, in_weight, out_weight, skip_gain, cotangent):
    total_frames, height, across, channels = frames.shape
    states_width = in_weight.shape[3]
    cell_norm = 1.0 / math.sqrt(total_frames * height * across)
    frame_norm = 1.0 / math.sqrt(height * across)
    skip_scale = skip_gain.astype(jnp.float32)
    in_pad = pad_frames(frames)
    drive_terms = conv_taps(in_pad, in_weight)

    def forward_step(state, inputs):
        decay_now, drive_now = inputs
        state = decay_now[None, None, :] * state + drive_now
        return (state, state)
    zero_state = jnp.zeros((height, across, states_width), jnp.float32)
    _, states = lax.scan(forward_step, zero_state, (decays, drive_terms))
    rounded = states.astype(jnp.bfloat16)
    state_pad = pad_frames(rounded)
    output_frames = (conv_taps(state_pad, out_weight) + skip_scale * frames.astype(jnp.float32)).astype(jnp.bfloat16)
    from_output = conv_taps(pad_frames(cotangent), flipped(out_weight))
    next_decay = jnp.concatenate([decays[1:], jnp.zeros((1, states_width), jnp.float32)], axis=0)

    def backward_step(adjoint_now, inputs):
        decay_next, from_now = inputs
        adjoint_now = from_now + decay_next[None, None, :] * adjoint_now
        return (adjoint_now, adjoint_now)
    _, adjoint = lax.scan(backward_step, zero_state, (next_decay, from_output), reverse=True)
    previous = jnp.concatenate([zero_state[None], states[:-1]], axis=0)
    decay_grad = lax.optimization_barrier(jnp.sum(adjoint * previous, axis=(1, 2))) * frame_norm
    adjoint_low = adjoint.astype(jnp.bfloat16)
    in_weight_grad = tap_grads(in_pad, adjoint_low) * cell_norm
    out_weight_grad = tap_grads(state_pad, cotangent) * cell_norm
    gain_grad = lax.optimization_barrier(jnp.sum(cotangent.astype(jnp.float32) * frames.astype(jnp.float32), axis=(0, 1, 2))) * cell_norm
    input_grad = (conv_taps(pad_frames(adjoint_low), flipped(in_weight)) + skip_scale * cotangent.astype(jnp.float32)).astype(jnp.bfloat16)
    return (output_frames, input_grad, in_weight_grad, out_weight_grad, gain_grad, decay_grad)
```

```python
import functools
import math

import jax
import jax.numpy as jnp
from jax import lax
from jax.experimental import pallas as pl
from jax.experimental.pallas import tpu as pltpu
from jax.sharding import PartitionSpec as P

F32 = jnp.float32
BF16 = jnp.bfloat16
MESH = pl.DeviceIdType.MESH


def dot_nn(a, b):
    return lax.dot_general(a, b, (((1,), (0,)), ((), ())), preferred_element_type=F32)


def dot_nt(a, b):
    return lax.dot_general(a, b, (((1,), (1,)), ((), ())), preferred_element_type=F32)


def dot_tn(a, b):
    return lax.dot_general(a, b, (((0,), (0,)), ((), ())), preferred_element_type=F32)


def put_shifted(cat, first, value, across):
    cells, width = value.shape
    rows = cells // across
    wide = value.astype(F32)
    column = lax.broadcasted_iota(jnp.int32, (rows, across, width), 1)
    left = pltpu.roll(wide, 1, 0).reshape(rows, across, width)
    right = pltpu.roll(wide, cells - 1, 0).reshape(rows, across, width)
    cat[first : first + rows, :, 0:width] = jnp.where(column == 0, 0.0, left).astype(BF16)
    cat[first : first + rows, :, width : 2 * width] = value.reshape(rows, across, width)
    cat[first : first + rows, :, 2 * width : 3 * width] = jnp.where(
        column == across - 1, 0.0, right
    ).astype(BF16)


def kernel(
    n_tm, n_rows, pp, cell_norm, frame_norm,
    frames, decays, in_w, out_w, gain, cot,
    y_out, dx_out, gin_out, gout_out, ggain_out, gdec_out,
    halo_s, halo_r, dec_s, dec_all, cat_f, cat_c,
    st_d, st_o, rc_d, rc_o, st32, out_s, out_j, dp_s, dp_r, got_s, got_j,
    halo2_s, halo2_r, cat_s, cat_j,
    grads, rs_r, quarter, rs_t, piece, full, sm_s, sm_r, sm2_s, sm2_r,
    halo_ss, halo_rs, halo2_ss, halo2_rs, dec_ss, dec_rs,
    a_ss, a_rs, b_ss, b_rs, r_ss, r_rs, t_ss, t_rs, gt_ss, gt_rs, gr_ss, gr_rs,
):
    tm = lax.axis_index("tm")
    row = lax.axis_index("rows")
    _, band, across, ch = frames.shape
    s_ch = in_w.shape[3]
    cells = band * across
    chunk = cells // n_tm
    qb = n_tm * pp

    def flat(ref):
        if chunk % 16 == 0:
            return ref[...].reshape(cells, s_ch)
        return ref[...].astype(F32).reshape(cells, s_ch).astype(BF16)

    def others(axis_n, me, body):
        def one(s, carry):
            body(lax.rem(me + s, axis_n))
            return carry

        lax.fori_loop(1, axis_n, one, 0)

    def tm_copy(src, dst, ss, rs, peer):
        return pltpu.make_async_remote_copy(
            src_ref=src, dst_ref=dst, send_sem=ss, recv_sem=rs,
            device_id={"tm": peer}, device_id_type=MESH,
        )

    def row_copy(src, dst, ss, rs, peer):
        return pltpu.make_async_remote_copy(
            src_ref=src, dst_ref=dst, send_sem=ss, recv_sem=rs,
            device_id={"rows": peer}, device_id_type=MESH,
        )

    has_low = row > 0
    has_high = row < n_rows - 1

    def halo_up(s, r, ss, rs):
        return row_copy(s.at[0], r.at[1], ss.at[0], rs.at[1], row - 1)

    def halo_down(s, r, ss, rs):
        return row_copy(s.at[1], r.at[0], ss.at[1], rs.at[0], row + 1)

    def halo_start(s, r, ss, rs):
        @pl.when(has_low)
        def _():
            halo_up(s, r, ss, rs).start()

        @pl.when(has_high)
        def _():
            halo_down(s, r, ss, rs).start()

        @pl.when(jnp.logical_not(has_low))
        def _():
            r[0] = jnp.zeros(r.shape[1:], r.dtype)

        @pl.when(jnp.logical_not(has_high))
        def _():
            r[1] = jnp.zeros(r.shape[1:], r.dtype)

    def halo_wait(s, r, ss, rs):
        @pl.when(has_low)
        def _():
            row_copy(s.at[0], r.at[0], ss.at[0], rs.at[0], row - 1).wait_recv()

        @pl.when(has_high)
        def _():
            row_copy(s.at[1], r.at[1], ss.at[1], rs.at[1], row + 1).wait_recv()

    def halo_end(s, r, ss, rs):
        @pl.when(has_low)
        def _():
            halo_up(s, r, ss, rs).wait_send()

        @pl.when(has_high)
        def _():
            halo_down(s, r, ss, rs).wait_send()

    barrier = pltpu.get_barrier_semaphore()
    others(n_tm, tm, lambda p: pl.semaphore_signal(
        barrier, inc=1, device_id={"tm": p}, device_id_type=MESH))
    others(n_rows, row, lambda p: pl.semaphore_signal(
        barrier, inc=1, device_id={"rows": p}, device_id_type=MESH))
    halo_s[0, 0] = frames[0, 0]
    halo_s[0, 1] = cot[0, 0]
    halo_s[1, 0] = frames[0, band - 1]
    halo_s[1, 1] = cot[0, band - 1]
    own_decay = jnp.broadcast_to(decays[...], (8, s_ch))
    dec_s[...] = own_decay
    dec_all[tm] = own_decay
    pl.semaphore_wait(barrier, n_tm - 1 + n_rows - 1)

    halo_start(halo_s, halo_r, halo_ss, halo_rs)
    others(n_tm, tm, lambda p: tm_copy(
        dec_s, dec_all.at[tm], dec_ss.at[p], dec_rs.at[tm], p).start())

    frames_own = frames[0].reshape(cells, ch)
    cot_own = cot[0].reshape(cells, ch)
    put_shifted(cat_f, 1, frames_own, across)
    put_shifted(cat_c, 1, cot_own, across)
    gain_sum = jnp.sum(
        frames_own.astype(F32) * cot_own.astype(F32), axis=0, keepdims=True) * cell_norm
    sm_s[...] = jnp.zeros(sm_s.shape, F32)
    sm_s[1:2, 0:ch] = gain_sum

    halo_wait(halo_s, halo_r, halo_ss, halo_rs)
    put_shifted(cat_f, 0, halo_r[0, 0], across)
    put_shifted(cat_f, band + 1, halo_r[1, 0], across)
    put_shifted(cat_c, 0, halo_r[0, 1], across)
    put_shifted(cat_c, band + 1, halo_r[1, 1], across)

    acc = None
    for i in range(3):
        term = dot_nn(cat_f[i : i + band].reshape(cells, 3 * ch), in_w[i].reshape(3 * ch, s_ch))
        acc = term if acc is None else acc + term
    st_d[...] = acc.reshape(n_tm, chunk, s_ch).astype(BF16)
    others(n_tm, tm, lambda p: tm_copy(
        st_d.at[p], rc_d.at[tm], a_ss.at[0, p], a_rs.at[0, tm], p).start())
    rc_d[tm] = st_d[tm]

    acc = None
    for i in range(3):
        for j in range(3):
            window = cat_c[i : i + band, :, j * ch : (j + 1) * ch].reshape(cells, ch)
            term = dot_nt(window, out_w[2 - i, 2 - j])
            acc = term if acc is None else acc + term
    st_o[...] = acc.reshape(n_tm, chunk, s_ch).astype(BF16)
    others(n_tm, tm, lambda p: tm_copy(
        st_o.at[p], rc_o.at[tm], a_ss.at[1, p], a_rs.at[1, tm], p).start())
    rc_o[tm] = st_o[tm]

    others(n_tm, tm, lambda p: tm_copy(
        dec_s, dec_all.at[p], dec_ss.at[p], dec_rs.at[p], p).wait_recv())
    others(n_tm, tm, lambda p: tm_copy(
        st_d.at[p], rc_d.at[p], a_ss.at[0, p], a_rs.at[0, p], p).wait_recv())

    def forward(t, state):
        state = dec_all[t][0:1] * state + rc_d[t].astype(F32)
        st32[t + 1] = state
        out_s[t] = state.astype(BF16)
        return state

    st32[0] = jnp.zeros((chunk, s_ch), F32)
    lax.fori_loop(0, n_tm, forward, jnp.zeros((chunk, s_ch), F32))
    others(n_tm, tm, lambda p: tm_copy(
        out_s.at[p], got_s.at[tm], b_ss.at[0, p], b_rs.at[0, tm], p).start())
    got_s[tm] = out_s[tm]

    others(n_tm, tm, lambda p: tm_copy(
        st_o.at[p], rc_o.at[p], a_ss.at[1, p], a_rs.at[1, p], p).wait_recv())

    def backward(turn, carried):
        t = n_tm - 1 - turn
        adjoint = rc_o[t].astype(F32) + carried
        out_j[t] = adjoint.astype(BF16)
        dp_s[t] = jnp.sum((adjoint * st32[t]).reshape(chunk // 8, 8, s_ch), axis=0)
        return dec_all[t][0:1] * adjoint

    lax.fori_loop(0, n_tm, backward, jnp.zeros((chunk, s_ch), F32))
    others(n_tm, tm, lambda p: tm_copy(
        out_j.at[p], got_j.at[tm], b_ss.at[1, p], b_rs.at[1, tm], p).start())
    others(n_tm, tm, lambda p: tm_copy(
        dp_s.at[p], dp_r.at[tm], b_ss.at[2, p], b_rs.at[2, tm], p).start())
    got_j[tm] = out_j[tm]
    dp_r[tm] = dp_s[tm]

    others(n_tm, tm, lambda p: tm_copy(
        out_s.at[p], got_s.at[p], b_ss.at[0, p], b_rs.at[0, p], p).wait_recv())
    states_own = flat(got_s)
    for i in range(3):
        value = dot_tn(states_own, cat_c[i : i + band].reshape(cells, 3 * ch)) * cell_norm
        for j in range(3):
            tap = (2 - i) * 3 + 2 - j
            base = 9 * s_ch * ch // 2048 + tap * (s_ch // 16)
            grads[base : base + s_ch // 16] = (
                value[:, j * ch : (j + 1) * ch].astype(BF16).reshape(s_ch // 16, 16, ch))

    others(n_tm, tm, lambda p: tm_copy(
        out_j.at[p], got_j.at[p], b_ss.at[1, p], b_rs.at[1, p], p).wait_recv())
    adj_own = flat(got_j)
    halo2_s[0, 0] = states_own[0:across]
    halo2_s[0, 1] = adj_own[0:across]
    halo2_s[1, 0] = states_own[cells - across :]
    halo2_s[1, 1] = adj_own[cells - across :]
    halo_start(halo2_s, halo2_r, halo2_ss, halo2_rs)
    blocks = 3 * ch // 16
    for i in range(3):
        value = dot_tn(cat_f[i : i + band].reshape(cells, 3 * ch), adj_own) * cell_norm
        for h in range(s_ch // 128):
            base = (h * 3 + i) * blocks
            grads[base : base + blocks] = (
                value[:, h * 128 : (h + 1) * 128].astype(BF16).reshape(blocks, 16, 128))
    used = 18 * ch * s_ch // 2048
    if used < n_rows * qb:
        grads[used:] = jnp.zeros((n_rows * qb - used, 16, 128), BF16)
    others(n_tm, tm, lambda p: tm_copy(
        dp_s.at[p], dp_r.at[p], b_ss.at[2, p], b_rs.at[2, p], p).wait_recv())
    sm_s[0:1] = jnp.sum(jnp.sum(dp_r[...], axis=0), axis=0, keepdims=True) * frame_norm
    sm_r[row] = sm_s[...]

    def rs_row(p, slot):
        return row_copy(
            grads.at[pl.ds(p * qb, qb)], rs_r.at[slot], r_ss.at[0, p], r_rs.at[0, slot], p)

    def small_row(p, slot):
        return row_copy(sm_s, sm_r.at[slot], r_ss.at[1, p], r_rs.at[1, slot], p)

    others(n_rows, row, lambda p: rs_row(p, row).start())
    others(n_rows, row, lambda p: small_row(p, row).start())
    rs_r[row] = grads[pl.ds(row * qb, qb)]

    halo_wait(halo2_s, halo2_r, halo2_ss, halo2_rs)
    put_shifted(cat_s, 0, halo2_r[0, 0], across)
    put_shifted(cat_s, 1, states_own, across)
    put_shifted(cat_s, band + 1, halo2_r[1, 0], across)
    put_shifted(cat_j, 0, halo2_r[0, 1], across)
    put_shifted(cat_j, 1, adj_own, across)
    put_shifted(cat_j, band + 1, halo2_r[1, 1], across)
    acc = gain[...] * frames_own.astype(F32)
    for i in range(3):
        acc = acc + dot_nn(
            cat_s[i : i + band].reshape(cells, 3 * s_ch), out_w[i].reshape(3 * s_ch, ch))
    y_out[0] = acc.astype(BF16).reshape(band, across, ch)
    acc = gain[...] * cot_own.astype(F32)
    for i in range(3):
        for j in range(3):
            window = cat_j[i : i + band, :, j * s_ch : (j + 1) * s_ch].reshape(cells, s_ch)
            acc = acc + dot_nt(window, in_w[2 - i, 2 - j])
    dx_out[0] = acc.astype(BF16).reshape(band, across, ch)

    others(n_rows, row, lambda p: rs_row(p, p).wait_recv())
    others(n_rows, row, lambda p: small_row(p, p).wait_recv())
    quarter[...] = jnp.sum(rs_r[...].astype(F32), axis=0).astype(BF16)
    small = jnp.sum(sm_r[...], axis=0)
    sm2_s[...] = small
    sm2_r[tm] = small
    gdec_out[...] = small[0:1]

    def rs_tm(p, slot):
        return tm_copy(
            quarter.at[pl.ds(p * pp, pp)], rs_t.at[slot], t_ss.at[0, p], t_rs.at[0, slot], p)

    def small_tm(p, slot):
        return tm_copy(sm2_s, sm2_r.at[slot], t_ss.at[1, p], t_rs.at[1, slot], p)

    others(n_tm, tm, lambda p: rs_tm(p, tm).start())
    others(n_tm, tm, lambda p: small_tm(p, tm).start())
    rs_t[tm] = quarter[pl.ds(tm * pp, pp)]
    others(n_tm, tm, lambda p: rs_tm(p, p).wait_recv())
    total = jnp.sum(rs_t[...].astype(F32), axis=0).astype(BF16)
    piece[...] = total
    full[row, tm] = total

    def ag_tm(p, slot):
        return tm_copy(piece, full.at[row, slot], gt_ss.at[p], gt_rs.at[slot], p)

    def ag_row(p, slot):
        return row_copy(full.at[row], full.at[slot], gr_ss.at[p], gr_rs.at[slot], p)

    others(n_tm, tm, lambda p: ag_tm(p, tm).start())
    others(n_tm, tm, lambda p: small_tm(p, p).wait_recv())
    ggain_out[...] = jnp.sum(sm2_r[...], axis=0)[1:2, 0:ch]
    others(n_tm, tm, lambda p: ag_tm(p, p).wait_recv())
    others(n_rows, row, lambda p: ag_row(p, row).start())
    others(n_rows, row, lambda p: ag_row(p, p).wait_recv())

    everything = full[...].reshape(n_rows * qb, 16, 128)
    half = 9 * ch // 16
    for h in range(s_ch // 128):
        gin_out[:, h * 128 : (h + 1) * 128] = (
            everything[h * half : (h + 1) * half].astype(F32).reshape(9 * ch, 128))
    base = 9 * s_ch * ch // 2048
    gout_out[...] = everything[base : 2 * base].astype(F32).reshape(9 * s_ch, ch)

    halo_end(halo_s, halo_r, halo_ss, halo_rs)
    halo_end(halo2_s, halo2_r, halo2_ss, halo2_rs)

    def tm_sends(p):
        tm_copy(dec_s, dec_all.at[tm], dec_ss.at[p], dec_rs.at[tm], p).wait_send()
        tm_copy(st_d.at[p], rc_d.at[tm], a_ss.at[0, p], a_rs.at[0, tm], p).wait_send()
        tm_copy(st_o.at[p], rc_o.at[tm], a_ss.at[1, p], a_rs.at[1, tm], p).wait_send()
        tm_copy(out_s.at[p], got_s.at[tm], b_ss.at[0, p], b_rs.at[0, tm], p).wait_send()
        tm_copy(out_j.at[p], got_j.at[tm], b_ss.at[1, p], b_rs.at[1, tm], p).wait_send()
        tm_copy(dp_s.at[p], dp_r.at[tm], b_ss.at[2, p], b_rs.at[2, tm], p).wait_send()
        rs_tm(p, tm).wait_send()
        small_tm(p, tm).wait_send()
        ag_tm(p, tm).wait_send()

    def row_sends(p):
        rs_row(p, row).wait_send()
        small_row(p, row).wait_send()
        ag_row(p, row).wait_send()

    others(n_tm, tm, tm_sends)
    others(n_rows, row, row_sends)


def on_device(n_tm, n_rows, frames, decays, in_weight, out_weight, skip_gain, cotangent):
    frame_count, band, across, ch = frames.shape
    s_ch = in_weight.shape[3]
    cells = band * across
    assert frame_count == 1 and cells % (8 * n_tm) == 0
    assert ch == 128 and s_ch % 128 == 0 and across % 16 == 0
    cell_norm = 1.0 / math.sqrt(frame_count * n_tm * band * n_rows * across)
    frame_norm = 1.0 / math.sqrt(band * n_rows * across)
    chunk = cells // n_tm
    used = 18 * ch * s_ch // 2048
    pp = -(-used // (n_tm * n_rows))
    vmem = pltpu.VMEM
    parts = lambda kind: vmem((n_tm, chunk, s_ch), kind)
    dma = pltpu.SemaphoreType.DMA
    scratch = [
        vmem((2, 2, across, ch), BF16), vmem((2, 2, across, ch), BF16),
        vmem((8, s_ch), F32), vmem((n_tm, 8, s_ch), F32),
        vmem((band + 2, across, 3 * ch), BF16), vmem((band + 2, across, 3 * ch), BF16),
        parts(BF16), parts(BF16), parts(BF16), parts(BF16),
        vmem((n_tm + 1, chunk, s_ch), F32),
        parts(BF16), parts(BF16),
        vmem((n_tm, 8, s_ch), F32), vmem((n_tm, 8, s_ch), F32),
        parts(BF16), parts(BF16),
        vmem((2, 2, across, s_ch), BF16), vmem((2, 2, across, s_ch), BF16),
        vmem((band + 2, across, 3 * s_ch), BF16), vmem((band + 2, across, 3 * s_ch), BF16),
        vmem((n_rows * n_tm * pp, 16, 128), BF16),
        vmem((n_rows, n_tm * pp, 16, 128), BF16),
        vmem((n_tm * pp, 16, 128), BF16),
        vmem((n_tm, pp, 16, 128), BF16),
        vmem((pp, 16, 128), BF16),
        vmem((n_rows, n_tm, pp, 16, 128), BF16),
        vmem((8, s_ch), F32), vmem((n_rows, 8, s_ch), F32),
        vmem((8, s_ch), F32), vmem((n_tm, 8, s_ch), F32),
        dma((2,)), dma((2,)), dma((2,)), dma((2,)), dma((n_tm,)), dma((n_tm,)),
        dma((2, n_tm)), dma((2, n_tm)), dma((3, n_tm)), dma((3, n_tm)),
        dma((2, n_rows)), dma((2, n_rows)), dma((2, n_tm)), dma((2, n_tm)),
        dma((n_tm,)), dma((n_tm,)), dma((n_rows,)), dma((n_rows,)),
    ]
    y, dx, gin, gout, ggain, gdec = pl.pallas_call(
        functools.partial(kernel, n_tm, n_rows, pp, cell_norm, frame_norm),
        out_shape=(
            jax.ShapeDtypeStruct(frames.shape, BF16),
            jax.ShapeDtypeStruct(frames.shape, BF16),
            jax.ShapeDtypeStruct((9 * ch, s_ch), F32),
            jax.ShapeDtypeStruct((9 * s_ch, ch), F32),
            jax.ShapeDtypeStruct((1, ch), F32),
            jax.ShapeDtypeStruct((1, s_ch), F32),
        ),
        in_specs=[pl.BlockSpec(memory_space=pltpu.VMEM)] * 6,
        out_specs=[pl.BlockSpec(memory_space=pltpu.VMEM)] * 6,
        scratch_shapes=scratch,
        compiler_params=pltpu.CompilerParams(
            collective_id=0, has_side_effects=True, vmem_limit_bytes=48 * 2**20),
    )(frames, decays, in_weight, out_weight, skip_gain.reshape(1, ch), cotangent)
    return (y, dx, gin.reshape(3, 3, ch, s_ch), gout.reshape(3, 3, s_ch, ch),
            ggain.reshape(ch), gdec)


def solution(mesh):
    in_specs = (
        P("tm", "rows", None, None),
        P("tm", None),
        P(),
        P(),
        P(),
        P("tm", "rows", None, None),
    )
    out_specs = (
        P("tm", "rows", None, None),
        P("tm", "rows", None, None),
        P(),
        P(),
        P(),
        P("tm", None),
    )
    body = functools.partial(on_device, mesh.shape["tm"], mesh.shape["rows"])
    return jax.shard_map(
        body, mesh=mesh, in_specs=in_specs, out_specs=out_specs, check_vma=False
    )
```

```python
import functools
import math

import jax
import jax.numpy as jnp
from jax import lax
from jax.experimental import pallas as pl
from jax.experimental.pallas import tpu as pltpu
from jax.sharding import PartitionSpec as P

F32 = jnp.float32
BF16 = jnp.bfloat16
MESH = pl.DeviceIdType.MESH


def dot_nn(a, b):
    return lax.dot_general(a, b, (((1,), (0,)), ((), ())), preferred_element_type=F32)


def dot_nt(a, b):
    return lax.dot_general(a, b, (((1,), (1,)), ((), ())), preferred_element_type=F32)


def dot_tn(a, b):
    return lax.dot_general(a, b, (((0,), (0,)), ((), ())), preferred_element_type=F32)


def put_shifted(cat, first, value, across):
    cells, width = value.shape
    rows = cells // across
    wide = value.astype(F32)
    column = lax.broadcasted_iota(jnp.int32, (rows, across, width), 1)
    left = pltpu.roll(wide, 1, 0).reshape(rows, across, width)
    right = pltpu.roll(wide, cells - 1, 0).reshape(rows, across, width)
    cat[first : first + rows, :, 0:width] = jnp.where(column == 0, 0.0, left).astype(BF16)
    cat[first : first + rows, :, width : 2 * width] = value.reshape(rows, across, width)
    cat[first : first + rows, :, 2 * width : 3 * width] = jnp.where(
        column == across - 1, 0.0, right
    ).astype(BF16)


def kernel(
    n_tm, n_rows, g, pa, pb, cell_norm, frame_norm,
    frames, decays, in_w, out_w, gain, cot,
    y_out, dx_out, gin_out, gout_out, ggain_out, gdec_out,
    halo_s, halo_r, dec_s, dec_all, cat_f, cat_c,
    st_d, st_o, rc_d, rc_o, st32, ad32, out_s, out_j, dp_s, dp_r, got_s, got_j,
    cf_s, cf_r, cb_s, cb_r,
    halo2_s, halo2_r, cat_s, cat_j,
    grads, rs_r, quarter, rs_t, piece, full,
    rb_t, eighth, rb_r, piece_b, full_b, sm_s, sm_r, sm2_s, sm2_r,
    halo_ss, halo_rs, halo2_ss, halo2_rs, dec_ss, dec_rs,
    a_ss, a_rs, b_ss, b_rs, r_ss, r_rs, t_ss, t_rs, gt_ss, gt_rs, gr_ss, gr_rs,
    bt_ss, bt_rs, br_ss, br_rs, hr_ss, hr_rs, ht_ss, ht_rs, c_ss, c_rs,
):
    tm = lax.axis_index("tm")
    row = lax.axis_index("rows")
    _, band, across, ch = frames.shape
    s_ch = in_w.shape[3]
    cells = band * across
    chunk = cells // g
    qa = n_tm * pa
    qb = n_rows * pb
    na = n_rows * qa
    groups = n_tm // g
    group = tm // g
    me = lax.rem(tm, g)
    first = group * g

    def flat(ref):
        if chunk % 16 == 0:
            return ref[...].reshape(cells, s_ch)
        return ref[...].astype(F32).reshape(cells, s_ch).astype(BF16)

    def others(axis_n, me, body):
        def one(s, carry):
            body(lax.rem(me + s, axis_n))
            return carry

        lax.fori_loop(1, axis_n, one, 0)

    def tm_copy(src, dst, ss, rs, peer):
        return pltpu.make_async_remote_copy(
            src_ref=src, dst_ref=dst, send_sem=ss, recv_sem=rs,
            device_id={"tm": peer}, device_id_type=MESH,
        )

    def g_copy(src, dst, ss, rs, peer):
        return tm_copy(src, dst, ss, rs, first + peer)

    def row_copy(src, dst, ss, rs, peer):
        return pltpu.make_async_remote_copy(
            src_ref=src, dst_ref=dst, send_sem=ss, recv_sem=rs,
            device_id={"rows": peer}, device_id_type=MESH,
        )

    has_low = row > 0
    has_high = row < n_rows - 1

    def halo_up(s, r, ss, rs):
        return row_copy(s.at[0], r.at[1], ss.at[0], rs.at[1], row - 1)

    def halo_down(s, r, ss, rs):
        return row_copy(s.at[1], r.at[0], ss.at[1], rs.at[0], row + 1)

    def halo_start(s, r, ss, rs):
        @pl.when(has_low)
        def _():
            halo_up(s, r, ss, rs).start()

        @pl.when(has_high)
        def _():
            halo_down(s, r, ss, rs).start()

        @pl.when(jnp.logical_not(has_low))
        def _():
            r[0] = jnp.zeros(r.shape[1:], r.dtype)

        @pl.when(jnp.logical_not(has_high))
        def _():
            r[1] = jnp.zeros(r.shape[1:], r.dtype)

    def halo_wait(s, r, ss, rs):
        @pl.when(has_low)
        def _():
            row_copy(s.at[0], r.at[0], ss.at[0], rs.at[0], row - 1).wait_recv()

        @pl.when(has_high)
        def _():
            row_copy(s.at[1], r.at[1], ss.at[1], rs.at[1], row + 1).wait_recv()

    def halo_end(s, r, ss, rs):
        @pl.when(has_low)
        def _():
            halo_up(s, r, ss, rs).wait_send()

        @pl.when(has_high)
        def _():
            halo_down(s, r, ss, rs).wait_send()

    barrier = pltpu.get_barrier_semaphore()
    others(n_tm, tm, lambda p: pl.semaphore_signal(
        barrier, inc=1, device_id={"tm": p}, device_id_type=MESH))
    others(n_rows, row, lambda p: pl.semaphore_signal(
        barrier, inc=1, device_id={"rows": p}, device_id_type=MESH))
    halo_s[0, 0] = frames[0, 0]
    halo_s[0, 1] = cot[0, 0]
    halo_s[1, 0] = frames[0, band - 1]
    halo_s[1, 1] = cot[0, band - 1]
    own_decay = jnp.broadcast_to(decays[...], (8, s_ch))
    dec_s[...] = own_decay
    dec_all[me] = own_decay
    pl.semaphore_wait(barrier, n_tm - 1 + n_rows - 1)

    halo_start(halo_s, halo_r, halo_ss, halo_rs)
    others(g, me, lambda p: g_copy(
        dec_s, dec_all.at[me], dec_ss.at[p], dec_rs.at[me], p).start())

    frames_own = frames[0].reshape(cells, ch)
    cot_own = cot[0].reshape(cells, ch)
    put_shifted(cat_f, 1, frames_own, across)
    put_shifted(cat_c, 1, cot_own, across)
    gain_sum = jnp.sum(
        frames_own.astype(F32) * cot_own.astype(F32), axis=0, keepdims=True) * cell_norm
    sm_s[...] = jnp.zeros(sm_s.shape, F32)
    sm_s[1:2, 0:ch] = gain_sum

    halo_wait(halo_s, halo_r, halo_ss, halo_rs)
    put_shifted(cat_f, 0, halo_r[0, 0], across)
    put_shifted(cat_f, band + 1, halo_r[1, 0], across)
    put_shifted(cat_c, 0, halo_r[0, 1], across)
    put_shifted(cat_c, band + 1, halo_r[1, 1], across)

    acc = None
    for i in range(3):
        term = dot_nn(cat_f[i : i + band].reshape(cells, 3 * ch), in_w[i].reshape(3 * ch, s_ch))
        acc = term if acc is None else acc + term
    st_d[...] = acc.reshape(g, chunk, s_ch).astype(BF16)
    others(g, me, lambda p: g_copy(
        st_d.at[p], rc_d.at[me], a_ss.at[0, p], a_rs.at[0, me], p).start())
    rc_d[me] = st_d[me]

    acc = None
    for i in range(3):
        for j in range(3):
            window = cat_c[i : i + band, :, j * ch : (j + 1) * ch].reshape(cells, ch)
            term = dot_nt(window, out_w[2 - i, 2 - j])
            acc = term if acc is None else acc + term
    st_o[...] = acc.reshape(g, chunk, s_ch).astype(BF16)
    others(g, me, lambda p: g_copy(
        st_o.at[p], rc_o.at[me], a_ss.at[1, p], a_rs.at[1, me], p).start())
    rc_o[me] = st_o[me]

    others(g, me, lambda p: g_copy(
        dec_s, dec_all.at[p], dec_ss.at[p], dec_rs.at[p], p).wait_recv())
    others(g, me, lambda p: g_copy(
        st_d.at[p], rc_d.at[p], a_ss.at[0, p], a_rs.at[0, p], p).wait_recv())
    zero = jnp.zeros((chunk, s_ch), F32)

    def carry_f():
        return tm_copy(cf_s, cf_r, c_ss.at[0], c_rs.at[0], tm + g)

    def carry_b():
        return tm_copy(cb_s, cb_r, c_ss.at[1], c_rs.at[1], tm - g)

    has_before = group > 0
    has_after = group < groups - 1

    def forward(t, state):
        state = dec_all[t][0:1] * state + rc_d[t].astype(F32)
        st32[t + 1] = state
        return state

    state_end = lax.fori_loop(0, g, forward, zero)

    @pl.when(jnp.logical_not(has_before))
    def _():
        cf_r[...] = jnp.zeros(cf_r.shape, BF16)
        if groups > 1:
            cf_s[...] = state_end.astype(BF16)
            carry_f().start()

    others(g, me, lambda p: g_copy(
        st_o.at[p], rc_o.at[p], a_ss.at[1, p], a_rs.at[1, p], p).wait_recv())

    def backward(turn, carried):
        t = g - 1 - turn
        adjoint = rc_o[t].astype(F32) + carried
        ad32[t] = adjoint
        return dec_all[t][0:1] * adjoint

    adjoint_end = lax.fori_loop(0, g, backward, zero)

    @pl.when(jnp.logical_not(has_after))
    def _():
        cb_r[...] = jnp.zeros(cb_r.shape, BF16)
        if groups > 1:
            cb_s[...] = adjoint_end.astype(BF16)
            carry_b().start()

    decay_all = dec_all[0][0:1]
    for t in range(1, g):
        decay_all = decay_all * dec_all[t][0:1]

    @pl.when(has_before)
    def _():
        tm_copy(cf_s, cf_r, c_ss.at[0], c_rs.at[0], tm - g).wait_recv()

        @pl.when(has_after)
        def _():
            cf_s[...] = (st32[g] + decay_all * cf_r[...].astype(F32)).astype(BF16)
            carry_f().start()

    def forward_fix(t, carried):
        carried = dec_all[t][0:1] * carried
        state = st32[t + 1] + carried
        st32[t + 1] = state
        out_s[t] = state.astype(BF16)
        return carried

    state_in = cf_r[...].astype(F32)
    st32[0] = state_in
    lax.fori_loop(0, g, forward_fix, state_in)
    others(g, me, lambda p: g_copy(
        out_s.at[p], got_s.at[me], b_ss.at[0, p], b_rs.at[0, me], p).start())
    got_s[me] = out_s[me]

    @pl.when(has_after)
    def _():
        tm_copy(cb_s, cb_r, c_ss.at[1], c_rs.at[1], tm + g).wait_recv()

        @pl.when(has_before)
        def _():
            cb_s[...] = (
                dec_all[0][0:1] * ad32[0] + decay_all * cb_r[...].astype(F32)).astype(BF16)
            carry_b().start()

    def backward_fix(turn, carried):
        t = g - 1 - turn
        adjoint = ad32[t] + carried
        out_j[t] = adjoint.astype(BF16)
        dp_s[t] = jnp.sum((adjoint * st32[t]).reshape(chunk // 8, 8, s_ch), axis=0)
        return dec_all[t][0:1] * carried

    lax.fori_loop(0, g, backward_fix, cb_r[...].astype(F32))
    others(g, me, lambda p: g_copy(
        out_j.at[p], got_j.at[me], b_ss.at[1, p], b_rs.at[1, me], p).start())
    others(g, me, lambda p: g_copy(
        dp_s.at[p], dp_r.at[me], b_ss.at[2, p], b_rs.at[2, me], p).start())
    got_j[me] = out_j[me]
    dp_r[me] = dp_s[me]

    def rs_row(p, slot):
        return row_copy(
            grads.at[pl.ds(p * qa, qa)], rs_r.at[slot], r_ss.at[0, p], r_rs.at[0, slot], p)

    def small_row(p, slot):
        return row_copy(sm_s, sm_r.at[slot], r_ss.at[1, p], r_rs.at[1, slot], p)

    def rb_tm(p, slot):
        return tm_copy(
            grads.at[pl.ds(na + p * qb, qb)], rb_t.at[slot], bt_ss.at[p], bt_rs.at[slot], p)

    def rb_row(p, slot):
        return row_copy(
            eighth.at[pl.ds(p * pb, pb)], rb_r.at[slot], br_ss.at[p], br_rs.at[slot], p)

    def hb_row(p, slot):
        return row_copy(piece_b, full_b.at[tm, slot], hr_ss.at[p], hr_rs.at[slot], p)

    def hb_tm(p, slot):
        return tm_copy(full_b.at[tm], full_b.at[slot], ht_ss.at[p], ht_rs.at[slot], p)

    section = 9 * s_ch * ch // 2048
    early = section // qa

    def rs_early(p):
        @pl.when(p < early)
        def _():
            rs_row(p, row).start()

    def rs_late(p):
        @pl.when(p >= early)
        def _():
            rs_row(p, row).start()

    others(g, me, lambda p: g_copy(
        out_s.at[p], got_s.at[p], b_ss.at[0, p], b_rs.at[0, p], p).wait_recv())
    states_own = flat(got_s)
    for i in range(3):
        value = dot_tn(states_own, cat_c[i : i + band].reshape(cells, 3 * ch)) * cell_norm
        for j in range(3):
            tap = (2 - i) * 3 + 2 - j
            base = tap * (s_ch // 16)
            grads[base : base + s_ch // 16] = (
                value[:, j * ch : (j + 1) * ch].astype(BF16).reshape(s_ch // 16, 16, ch))
    others(n_rows, row, rs_early)

    others(g, me, lambda p: g_copy(
        out_j.at[p], got_j.at[p], b_ss.at[1, p], b_rs.at[1, p], p).wait_recv())
    adj_own = flat(got_j)
    halo2_s[0, 0] = states_own[0:across]
    halo2_s[0, 1] = adj_own[0:across]
    halo2_s[1, 0] = states_own[cells - across :]
    halo2_s[1, 1] = adj_own[cells - across :]
    halo_start(halo2_s, halo2_r, halo2_ss, halo2_rs)
    blocks = 3 * ch // 16
    for i in range(3):
        value = dot_tn(cat_f[i : i + band].reshape(cells, 3 * ch), adj_own) * cell_norm
        for h in range(s_ch // 128):
            base = section + (h * 3 + i) * blocks
            grads[base : base + blocks] = (
                value[:, h * 128 : (h + 1) * 128].astype(BF16).reshape(blocks, 16, 128))
    if 2 * section < na + n_tm * qb:
        grads[2 * section :] = jnp.zeros((na + n_tm * qb - 2 * section, 16, 128), BF16)
    others(n_rows, row, rs_late)
    others(n_tm, tm, lambda p: rb_tm(p, tm).start())
    rs_r[row] = grads[pl.ds(row * qa, qa)]
    rb_t[tm] = grads[pl.ds(na + tm * qb, qb)]
    others(g, me, lambda p: g_copy(
        dp_s.at[p], dp_r.at[p], b_ss.at[2, p], b_rs.at[2, p], p).wait_recv())
    sm_s[0:1] = jnp.sum(jnp.sum(dp_r[...], axis=0), axis=0, keepdims=True) * frame_norm
    sm_r[row] = sm_s[...]
    others(n_rows, row, lambda p: small_row(p, row).start())

    halo_wait(halo2_s, halo2_r, halo2_ss, halo2_rs)
    put_shifted(cat_s, 0, halo2_r[0, 0], across)
    put_shifted(cat_s, 1, states_own, across)
    put_shifted(cat_s, band + 1, halo2_r[1, 0], across)
    put_shifted(cat_j, 0, halo2_r[0, 1], across)
    put_shifted(cat_j, 1, adj_own, across)
    put_shifted(cat_j, band + 1, halo2_r[1, 1], across)
    acc = gain[...] * frames_own.astype(F32)
    for i in range(3):
        acc = acc + dot_nn(
            cat_s[i : i + band].reshape(cells, 3 * s_ch), out_w[i].reshape(3 * s_ch, ch))
    y_out[0] = acc.astype(BF16).reshape(band, across, ch)
    acc = gain[...] * cot_own.astype(F32)
    for i in range(3):
        for j in range(3):
            window = cat_j[i : i + band, :, j * s_ch : (j + 1) * s_ch].reshape(cells, s_ch)
            acc = acc + dot_nt(window, in_w[2 - i, 2 - j])
    dx_out[0] = acc.astype(BF16).reshape(band, across, ch)

    others(n_rows, row, lambda p: rs_row(p, p).wait_recv())
    others(n_rows, row, lambda p: small_row(p, p).wait_recv())
    quarter[...] = jnp.sum(rs_r[...].astype(F32), axis=0).astype(BF16)
    small = jnp.sum(sm_r[...], axis=0)
    sm2_s[...] = small
    sm2_r[tm] = small
    gdec_out[...] = small[0:1]

    def rs_tm(p, slot):
        return tm_copy(
            quarter.at[pl.ds(p * pa, pa)], rs_t.at[slot], t_ss.at[0, p], t_rs.at[0, slot], p)

    def small_tm(p, slot):
        return tm_copy(sm2_s, sm2_r.at[slot], t_ss.at[1, p], t_rs.at[1, slot], p)

    others(n_tm, tm, lambda p: rs_tm(p, tm).start())
    others(n_tm, tm, lambda p: small_tm(p, tm).start())
    others(n_tm, tm, lambda p: rb_tm(p, p).wait_recv())
    eighth[...] = jnp.sum(rb_t[...].astype(F32), axis=0).astype(BF16)
    others(n_rows, row, lambda p: rb_row(p, row).start())
    rb_r[row] = eighth[pl.ds(row * pb, pb)]
    rs_t[tm] = quarter[pl.ds(tm * pa, pa)]
    others(n_tm, tm, lambda p: rs_tm(p, p).wait_recv())
    total = jnp.sum(rs_t[...].astype(F32), axis=0).astype(BF16)
    piece[...] = total
    full[row, tm] = total

    def ag_tm(p, slot):
        return tm_copy(piece, full.at[row, slot], gt_ss.at[p], gt_rs.at[slot], p)

    def ag_row(p, slot):
        return row_copy(full.at[row], full.at[slot], gr_ss.at[p], gr_rs.at[slot], p)

    others(n_tm, tm, lambda p: ag_tm(p, tm).start())
    others(n_rows, row, lambda p: rb_row(p, p).wait_recv())
    total_b = jnp.sum(rb_r[...].astype(F32), axis=0).astype(BF16)
    piece_b[...] = total_b
    full_b[tm, row] = total_b
    others(n_rows, row, lambda p: hb_row(p, row).start())
    others(n_tm, tm, lambda p: small_tm(p, p).wait_recv())
    ggain_out[...] = jnp.sum(sm2_r[...], axis=0)[1:2, 0:ch]
    others(n_tm, tm, lambda p: ag_tm(p, p).wait_recv())
    others(n_rows, row, lambda p: ag_row(p, row).start())
    others(n_rows, row, lambda p: hb_row(p, p).wait_recv())
    others(n_tm, tm, lambda p: hb_tm(p, tm).start())
    others(n_rows, row, lambda p: ag_row(p, p).wait_recv())

    def emit(source, low, high):
        half = section * 128 // s_ch
        cuts = [(0, section)] + [
            (section + h * half, section + (h + 1) * half) for h in range(s_ch // 128)]
        for which, (begin, end) in enumerate(cuts):
            a, b = max(begin, low), min(end, high)
            if a >= b:
                continue
            value = source[a - low : b - low].astype(F32).reshape((b - a) * 16, 128)
            rows = slice((a - begin) * 16, (b - begin) * 16)
            if which == 0:
                gout_out[rows, :] = value
            else:
                gin_out[rows, (which - 1) * 128 : which * 128] = value

    emit(full[...].reshape(na, 16, 128), 0, na)
    others(n_tm, tm, lambda p: hb_tm(p, p).wait_recv())
    emit(full_b[...].reshape(n_tm * qb, 16, 128), na, na + n_tm * qb)

    halo_end(halo_s, halo_r, halo_ss, halo_rs)
    halo_end(halo2_s, halo2_r, halo2_ss, halo2_rs)

    if groups > 1:
        @pl.when(has_after)
        def _():
            carry_f().wait_send()

        @pl.when(has_before)
        def _():
            carry_b().wait_send()

    def g_sends(p):
        g_copy(dec_s, dec_all.at[me], dec_ss.at[p], dec_rs.at[me], p).wait_send()
        g_copy(st_d.at[p], rc_d.at[me], a_ss.at[0, p], a_rs.at[0, me], p).wait_send()
        g_copy(st_o.at[p], rc_o.at[me], a_ss.at[1, p], a_rs.at[1, me], p).wait_send()
        g_copy(out_s.at[p], got_s.at[me], b_ss.at[0, p], b_rs.at[0, me], p).wait_send()
        g_copy(out_j.at[p], got_j.at[me], b_ss.at[1, p], b_rs.at[1, me], p).wait_send()
        g_copy(dp_s.at[p], dp_r.at[me], b_ss.at[2, p], b_rs.at[2, me], p).wait_send()

    def tm_sends(p):
        rs_tm(p, tm).wait_send()
        small_tm(p, tm).wait_send()
        ag_tm(p, tm).wait_send()
        rb_tm(p, tm).wait_send()
        hb_tm(p, tm).wait_send()

    def row_sends(p):
        rs_row(p, row).wait_send()
        small_row(p, row).wait_send()
        ag_row(p, row).wait_send()
        rb_row(p, row).wait_send()
        hb_row(p, row).wait_send()

    others(g, me, g_sends)
    others(n_tm, tm, tm_sends)
    others(n_rows, row, row_sends)


def on_device(n_tm, n_rows, frames, decays, in_weight, out_weight, skip_gain, cotangent):
    frame_count, band, across, ch = frames.shape
    s_ch = in_weight.shape[3]
    cells = band * across
    assert frame_count == 1 and n_tm % 4 == 0 and cells % 32 == 0
    assert ch == 128 and s_ch % 128 == 0 and across % 16 == 0
    cell_norm = 1.0 / math.sqrt(frame_count * n_tm * band * n_rows * across)
    frame_norm = 1.0 / math.sqrt(band * n_rows * across)
    g = 4
    chunk = cells // g
    devices = n_tm * n_rows
    used = 18 * ch * s_ch // 2048
    pa = -(-2 * used // (3 * devices))
    pb = max(1, -(-(used - pa * devices) // devices))
    vmem = pltpu.VMEM
    parts = lambda kind: vmem((g, chunk, s_ch), kind)
    dma = pltpu.SemaphoreType.DMA
    scratch = [
        vmem((2, 2, across, ch), BF16), vmem((2, 2, across, ch), BF16),
        vmem((8, s_ch), F32), vmem((g, 8, s_ch), F32),
        vmem((band + 2, across, 3 * ch), BF16), vmem((band + 2, across, 3 * ch), BF16),
        parts(BF16), parts(BF16), parts(BF16), parts(BF16),
        vmem((g + 1, chunk, s_ch), F32), parts(F32),
        parts(BF16), parts(BF16),
        vmem((g, 8, s_ch), F32), vmem((g, 8, s_ch), F32),
        parts(BF16), parts(BF16),
        vmem((chunk, s_ch), BF16), vmem((chunk, s_ch), BF16),
        vmem((chunk, s_ch), BF16), vmem((chunk, s_ch), BF16),
        vmem((2, 2, across, s_ch), BF16), vmem((2, 2, across, s_ch), BF16),
        vmem((band + 2, across, 3 * s_ch), BF16), vmem((band + 2, across, 3 * s_ch), BF16),
        vmem((devices * (pa + pb), 16, 128), BF16),
        vmem((n_rows, n_tm * pa, 16, 128), BF16),
        vmem((n_tm * pa, 16, 128), BF16),
        vmem((n_tm, pa, 16, 128), BF16),
        vmem((pa, 16, 128), BF16),
        vmem((n_rows, n_tm, pa, 16, 128), BF16),
        vmem((n_tm, n_rows * pb, 16, 128), BF16),
        vmem((n_rows * pb, 16, 128), BF16),
        vmem((n_rows, pb, 16, 128), BF16),
        vmem((pb, 16, 128), BF16),
        vmem((n_tm, n_rows, pb, 16, 128), BF16),
        vmem((8, s_ch), F32), vmem((n_rows, 8, s_ch), F32),
        vmem((8, s_ch), F32), vmem((n_tm, 8, s_ch), F32),
        dma((2,)), dma((2,)), dma((2,)), dma((2,)), dma((g,)), dma((g,)),
        dma((2, g)), dma((2, g)), dma((3, g)), dma((3, g)),
        dma((2, n_rows)), dma((2, n_rows)), dma((2, n_tm)), dma((2, n_tm)),
        dma((n_tm,)), dma((n_tm,)), dma((n_rows,)), dma((n_rows,)),
        dma((n_tm,)), dma((n_tm,)), dma((n_rows,)), dma((n_rows,)),
        dma((n_rows,)), dma((n_rows,)), dma((n_tm,)), dma((n_tm,)), dma((2,)), dma((2,)),
    ]
    y, dx, gin, gout, ggain, gdec = pl.pallas_call(
        functools.partial(kernel, n_tm, n_rows, g, pa, pb, cell_norm, frame_norm),
        out_shape=(
            jax.ShapeDtypeStruct(frames.shape, BF16),
            jax.ShapeDtypeStruct(frames.shape, BF16),
            jax.ShapeDtypeStruct((9 * ch, s_ch), F32),
            jax.ShapeDtypeStruct((9 * s_ch, ch), F32),
            jax.ShapeDtypeStruct((1, ch), F32),
            jax.ShapeDtypeStruct((1, s_ch), F32),
        ),
        in_specs=[pl.BlockSpec(memory_space=pltpu.VMEM)] * 6,
        out_specs=[pl.BlockSpec(memory_space=pltpu.VMEM)] * 6,
        scratch_shapes=scratch,
        compiler_params=pltpu.CompilerParams(
            collective_id=0, has_side_effects=True, vmem_limit_bytes=48 * 2**20),
    )(frames, decays, in_weight, out_weight, skip_gain.reshape(1, ch), cotangent)
    return (y, dx, gin.reshape(3, 3, ch, s_ch), gout.reshape(3, 3, s_ch, ch),
            ggain.reshape(ch), gdec)


def solution(mesh):
    in_specs = (
        P("tm", "rows", None, None),
        P("tm", None),
        P(),
        P(),
        P(),
        P("tm", "rows", None, None),
    )
    out_specs = (
        P("tm", "rows", None, None),
        P("tm", "rows", None, None),
        P(),
        P(),
        P(),
        P("tm", None),
    )
    body = functools.partial(on_device, mesh.shape["tm"], mesh.shape["rows"])
    return jax.shard_map(
        body, mesh=mesh, in_specs=in_specs, out_specs=out_specs, check_vma=False
    )
```

```python
import functools
import math

import jax
import jax.numpy as jnp
from jax import lax
from jax.experimental import pallas as pl
from jax.experimental.pallas import tpu as pltpu
from jax.sharding import PartitionSpec as P

F32 = jnp.float32
BF16 = jnp.bfloat16
MESH = pl.DeviceIdType.MESH


def dot_nn(a, b):
    return lax.dot_general(a, b, (((1,), (0,)), ((), ())), preferred_element_type=F32)


def dot_nt(a, b):
    return lax.dot_general(a, b, (((1,), (1,)), ((), ())), preferred_element_type=F32)


def dot_tn(a, b):
    return lax.dot_general(a, b, (((0,), (0,)), ((), ())), preferred_element_type=F32)


def put_shifted(cat, first, value, across):
    cells, width = value.shape
    rows = cells // across
    wide = value.astype(F32)
    column = lax.broadcasted_iota(jnp.int32, (rows, across, width), 1)
    left = pltpu.roll(wide, 1, 0).reshape(rows, across, width)
    right = pltpu.roll(wide, cells - 1, 0).reshape(rows, across, width)
    cat[first : first + rows, :, 0:width] = jnp.where(column == 0, 0.0, left).astype(BF16)
    cat[first : first + rows, :, width : 2 * width] = value.reshape(rows, across, width)
    cat[first : first + rows, :, 2 * width : 3 * width] = jnp.where(
        column == across - 1, 0.0, right
    ).astype(BF16)


def kernel(
    n_tm, n_rows, g, pa, pb, cell_norm, frame_norm,
    frames, decays, in_w, out_w, gain, cot,
    y_out, dx_out, gin_out, gout_out, ggain_out, gdec_out,
    halo_s, halo_r, dec_s, dec_all, cat_f, cat_c,
    st_d, st_o, rc_d, rc_o, st32, ad32, out_s, out_j, dp_s, dp_r, got_s, got_j,
    cf_s, cf_r, cb_s, cb_r,
    halo2_s, halo2_r, cat_s, cat_j,
    grads, rs_r, quarter, rs_t, piece, full,
    rb_t, eighth, rb_r, piece_b, full_b, sm_s, sm_r, sm2_s, sm2_r,
    halo_ss, halo_rs, halo2_ss, halo2_rs, dec_ss, dec_rs,
    a_ss, a_rs, b_ss, b_rs, r_ss, r_rs, t_ss, t_rs, gt_ss, gt_rs, gr_ss, gr_rs,
    bt_ss, bt_rs, br_ss, br_rs, hr_ss, hr_rs, ht_ss, ht_rs, c_ss, c_rs,
):
    tm = lax.axis_index("tm")
    row = lax.axis_index("rows")
    _, band, across, ch = frames.shape
    s_ch = in_w.shape[3]
    cells = band * across
    chunk = cells // g
    qa = n_tm * pa
    qb = n_rows * pb
    na = n_rows * qa
    groups = n_tm // g
    group = tm // g
    me = lax.rem(tm, g)
    first = group * g

    def flat(ref):
        if chunk % 16 == 0:
            return ref[...].reshape(cells, s_ch)
        return ref[...].astype(F32).reshape(cells, s_ch).astype(BF16)

    def others(axis_n, me, body):
        def one(s, carry):
            body(lax.rem(me + s, axis_n))
            return carry

        lax.fori_loop(1, axis_n, one, 0)

    def tm_copy(src, dst, ss, rs, peer):
        return pltpu.make_async_remote_copy(
            src_ref=src, dst_ref=dst, send_sem=ss, recv_sem=rs,
            device_id={"tm": peer}, device_id_type=MESH,
        )

    def g_copy(src, dst, ss, rs, peer):
        return tm_copy(src, dst, ss, rs, first + peer)

    def row_copy(src, dst, ss, rs, peer):
        return pltpu.make_async_remote_copy(
            src_ref=src, dst_ref=dst, send_sem=ss, recv_sem=rs,
            device_id={"rows": peer}, device_id_type=MESH,
        )

    has_low = row > 0
    has_high = row < n_rows - 1

    def halo_up(s, r, ss, rs):
        return row_copy(s.at[0], r.at[1], ss.at[0], rs.at[1], row - 1)

    def halo_down(s, r, ss, rs):
        return row_copy(s.at[1], r.at[0], ss.at[1], rs.at[0], row + 1)

    def halo_start(s, r, ss, rs):
        @pl.when(has_low)
        def _():
            halo_up(s, r, ss, rs).start()

        @pl.when(has_high)
        def _():
            halo_down(s, r, ss, rs).start()

        @pl.when(jnp.logical_not(has_low))
        def _():
            r[0] = jnp.zeros(r.shape[1:], r.dtype)

        @pl.when(jnp.logical_not(has_high))
        def _():
            r[1] = jnp.zeros(r.shape[1:], r.dtype)

    def halo_wait(s, r, ss, rs):
        @pl.when(has_low)
        def _():
            row_copy(s.at[0], r.at[0], ss.at[0], rs.at[0], row - 1).wait_recv()

        @pl.when(has_high)
        def _():
            row_copy(s.at[1], r.at[1], ss.at[1], rs.at[1], row + 1).wait_recv()

    def halo_end(s, r, ss, rs):
        @pl.when(has_low)
        def _():
            halo_up(s, r, ss, rs).wait_send()

        @pl.when(has_high)
        def _():
            halo_down(s, r, ss, rs).wait_send()

    barrier = pltpu.get_barrier_semaphore()
    others(n_tm, tm, lambda p: pl.semaphore_signal(
        barrier, inc=1, device_id={"tm": p}, device_id_type=MESH))
    others(n_rows, row, lambda p: pl.semaphore_signal(
        barrier, inc=1, device_id={"rows": p}, device_id_type=MESH))
    halo_s[0, 0] = frames[0, 0]
    halo_s[0, 1] = cot[0, 0]
    halo_s[1, 0] = frames[0, band - 1]
    halo_s[1, 1] = cot[0, band - 1]
    own_decay = jnp.broadcast_to(decays[...], (8, s_ch))
    dec_s[...] = own_decay
    dec_all[me] = own_decay
    pl.semaphore_wait(barrier, n_tm - 1 + n_rows - 1)

    halo_start(halo_s, halo_r, halo_ss, halo_rs)
    others(g, me, lambda p: g_copy(
        dec_s, dec_all.at[me], dec_ss.at[p], dec_rs.at[me], p).start())

    frames_own = frames[0].reshape(cells, ch)
    cot_own = cot[0].reshape(cells, ch)
    put_shifted(cat_f, 1, frames_own, across)
    put_shifted(cat_c, 1, cot_own, across)
    gain_sum = jnp.sum(
        frames_own.astype(F32) * cot_own.astype(F32), axis=0, keepdims=True) * cell_norm
    sm_s[...] = jnp.zeros(sm_s.shape, F32)
    sm_s[1:2, 0:ch] = gain_sum

    halo_wait(halo_s, halo_r, halo_ss, halo_rs)
    put_shifted(cat_f, 0, halo_r[0, 0], across)
    put_shifted(cat_f, band + 1, halo_r[1, 0], across)
    put_shifted(cat_c, 0, halo_r[0, 1], across)
    put_shifted(cat_c, band + 1, halo_r[1, 1], across)

    acc = None
    for i in range(3):
        term = dot_nn(cat_f[i : i + band].reshape(cells, 3 * ch), in_w[i].reshape(3 * ch, s_ch))
        acc = term if acc is None else acc + term
    st_d[...] = acc.reshape(g, chunk, s_ch).astype(BF16)
    others(g, me, lambda p: g_copy(
        st_d.at[p], rc_d.at[me], a_ss.at[0, p], a_rs.at[0, me], p).start())
    rc_d[me] = st_d[me]

    acc = None
    for i in range(3):
        for j in range(3):
            window = cat_c[i : i + band, :, j * ch : (j + 1) * ch].reshape(cells, ch)
            term = dot_nt(window, out_w[2 - i, 2 - j])
            acc = term if acc is None else acc + term
    st_o[...] = acc.reshape(g, chunk, s_ch).astype(BF16)
    others(g, me, lambda p: g_copy(
        st_o.at[p], rc_o.at[me], a_ss.at[1, p], a_rs.at[1, me], p).start())
    rc_o[me] = st_o[me]

    others(g, me, lambda p: g_copy(
        dec_s, dec_all.at[p], dec_ss.at[p], dec_rs.at[p], p).wait_recv())
    others(g, me, lambda p: g_copy(
        st_d.at[p], rc_d.at[p], a_ss.at[0, p], a_rs.at[0, p], p).wait_recv())
    zero = jnp.zeros((chunk, s_ch), F32)

    def carry_f():
        return tm_copy(cf_s, cf_r, c_ss.at[0], c_rs.at[0], tm + g)

    def carry_b():
        return tm_copy(cb_s, cb_r, c_ss.at[1], c_rs.at[1], tm - g)

    has_before = group > 0
    has_after = group < groups - 1

    def forward(t, state):
        state = dec_all[t][0:1] * state + rc_d[t].astype(F32)
        st32[t + 1] = state
        return state

    state_end = lax.fori_loop(0, g, forward, zero)

    @pl.when(jnp.logical_not(has_before))
    def _():
        cf_r[...] = jnp.zeros(cf_r.shape, BF16)
        if groups > 1:
            cf_s[...] = state_end.astype(BF16)
            carry_f().start()

    others(g, me, lambda p: g_copy(
        st_o.at[p], rc_o.at[p], a_ss.at[1, p], a_rs.at[1, p], p).wait_recv())

    def backward(turn, carried):
        t = g - 1 - turn
        adjoint = rc_o[t].astype(F32) + carried
        ad32[t] = adjoint
        return dec_all[t][0:1] * adjoint

    adjoint_end = lax.fori_loop(0, g, backward, zero)

    @pl.when(jnp.logical_not(has_after))
    def _():
        cb_r[...] = jnp.zeros(cb_r.shape, BF16)
        if groups > 1:
            cb_s[...] = adjoint_end.astype(BF16)
            carry_b().start()

    decay_all = dec_all[0][0:1]
    for t in range(1, g):
        decay_all = decay_all * dec_all[t][0:1]

    @pl.when(has_before)
    def _():
        tm_copy(cf_s, cf_r, c_ss.at[0], c_rs.at[0], tm - g).wait_recv()

        @pl.when(has_after)
        def _():
            cf_s[...] = (st32[g] + decay_all * cf_r[...].astype(F32)).astype(BF16)
            carry_f().start()

    def forward_fix(t, carried):
        carried = dec_all[t][0:1] * carried
        state = st32[t + 1] + carried
        st32[t + 1] = state
        out_s[t] = state.astype(BF16)
        return carried

    state_in = cf_r[...].astype(F32)
    st32[0] = state_in
    lax.fori_loop(0, g, forward_fix, state_in)
    others(g, me, lambda p: g_copy(
        out_s.at[p], got_s.at[me], b_ss.at[0, p], b_rs.at[0, me], p).start())
    got_s[me] = out_s[me]

    @pl.when(has_after)
    def _():
        tm_copy(cb_s, cb_r, c_ss.at[1], c_rs.at[1], tm + g).wait_recv()

        @pl.when(has_before)
        def _():
            cb_s[...] = (
                dec_all[0][0:1] * ad32[0] + decay_all * cb_r[...].astype(F32)).astype(BF16)
            carry_b().start()

    def backward_fix(turn, carried):
        t = g - 1 - turn
        adjoint = ad32[t] + carried
        out_j[t] = adjoint.astype(BF16)
        dp_s[t] = jnp.sum((adjoint * st32[t]).reshape(chunk // 8, 8, s_ch), axis=0)
        return dec_all[t][0:1] * carried

    lax.fori_loop(0, g, backward_fix, cb_r[...].astype(F32))
    others(g, me, lambda p: g_copy(
        out_j.at[p], got_j.at[me], b_ss.at[1, p], b_rs.at[1, me], p).start())
    others(g, me, lambda p: g_copy(
        dp_s.at[p], dp_r.at[me], b_ss.at[2, p], b_rs.at[2, me], p).start())
    got_j[me] = out_j[me]
    dp_r[me] = dp_s[me]

    def rs_row(p, slot):
        return row_copy(
            grads.at[pl.ds(p * qa, qa)], rs_r.at[slot], r_ss.at[0, p], r_rs.at[0, slot], p)

    def small_row(p, slot):
        return row_copy(sm_s, sm_r.at[slot], r_ss.at[1, p], r_rs.at[1, slot], p)

    def rb_tm(p, slot):
        return tm_copy(
            grads.at[pl.ds(na + p * qb, qb)], rb_t.at[slot], bt_ss.at[p], bt_rs.at[slot], p)

    def rb_row(p, slot):
        return row_copy(
            eighth.at[pl.ds(p * pb, pb)], rb_r.at[slot], br_ss.at[p], br_rs.at[slot], p)

    def hb_row(p, slot):
        return row_copy(piece_b, full_b.at[tm, slot], hr_ss.at[p], hr_rs.at[slot], p)

    def hb_tm(p, slot):
        return tm_copy(full_b.at[tm], full_b.at[slot], ht_ss.at[p], ht_rs.at[slot], p)

    section = 9 * s_ch * ch // 2048
    early = section // qa

    def rs_early(p):
        @pl.when(p < early)
        def _():
            rs_row(p, row).start()

    def rs_late(p):
        @pl.when(p >= early)
        def _():
            rs_row(p, row).start()

    others(g, me, lambda p: g_copy(
        out_s.at[p], got_s.at[p], b_ss.at[0, p], b_rs.at[0, p], p).wait_recv())
    states_own = flat(got_s)
    for i in range(3):
        value = dot_tn(states_own, cat_c[i : i + band].reshape(cells, 3 * ch)) * cell_norm
        for j in range(3):
            tap = (2 - i) * 3 + 2 - j
            base = tap * (s_ch // 16)
            grads[base : base + s_ch // 16] = (
                value[:, j * ch : (j + 1) * ch].astype(BF16).reshape(s_ch // 16, 16, ch))
    others(n_rows, row, rs_early)

    others(g, me, lambda p: g_copy(
        out_j.at[p], got_j.at[p], b_ss.at[1, p], b_rs.at[1, p], p).wait_recv())
    adj_own = flat(got_j)
    halo2_s[0, 0] = states_own[0:across]
    halo2_s[0, 1] = adj_own[0:across]
    halo2_s[1, 0] = states_own[cells - across :]
    halo2_s[1, 1] = adj_own[cells - across :]
    halo_start(halo2_s, halo2_r, halo2_ss, halo2_rs)
    blocks = 3 * ch // 16
    for i in range(3):
        value = dot_tn(cat_f[i : i + band].reshape(cells, 3 * ch), adj_own) * cell_norm
        for h in range(s_ch // 128):
            base = section + (h * 3 + i) * blocks
            grads[base : base + blocks] = (
                value[:, h * 128 : (h + 1) * 128].astype(BF16).reshape(blocks, 16, 128))
    if 2 * section < na + n_tm * qb:
        grads[2 * section :] = jnp.zeros((na + n_tm * qb - 2 * section, 16, 128), BF16)
    others(n_rows, row, rs_late)
    others(n_tm, tm, lambda p: rb_tm(p, tm).start())
    rs_r[row] = grads[pl.ds(row * qa, qa)]
    rb_t[tm] = grads[pl.ds(na + tm * qb, qb)]
    others(g, me, lambda p: g_copy(
        dp_s.at[p], dp_r.at[p], b_ss.at[2, p], b_rs.at[2, p], p).wait_recv())
    sm_s[0:1] = jnp.sum(jnp.sum(dp_r[...], axis=0), axis=0, keepdims=True) * frame_norm
    sm_r[row] = sm_s[...]
    others(n_rows, row, lambda p: small_row(p, row).start())

    halo_wait(halo2_s, halo2_r, halo2_ss, halo2_rs)
    put_shifted(cat_s, 0, halo2_r[0, 0], across)
    put_shifted(cat_s, 1, states_own, across)
    put_shifted(cat_s, band + 1, halo2_r[1, 0], across)
    put_shifted(cat_j, 0, halo2_r[0, 1], across)
    put_shifted(cat_j, 1, adj_own, across)
    put_shifted(cat_j, band + 1, halo2_r[1, 1], across)
    acc = gain[...] * frames_own.astype(F32)
    for i in range(3):
        acc = acc + dot_nn(
            cat_s[i : i + band].reshape(cells, 3 * s_ch), out_w[i].reshape(3 * s_ch, ch))
    y_out[0] = acc.astype(BF16).reshape(band, across, ch)
    acc = gain[...] * cot_own.astype(F32)
    for i in range(3):
        for j in range(3):
            window = cat_j[i : i + band, :, j * s_ch : (j + 1) * s_ch].reshape(cells, s_ch)
            acc = acc + dot_nt(window, in_w[2 - i, 2 - j])
    dx_out[0] = acc.astype(BF16).reshape(band, across, ch)

    others(n_rows, row, lambda p: rs_row(p, p).wait_recv())
    others(n_rows, row, lambda p: small_row(p, p).wait_recv())
    quarter[...] = jnp.sum(rs_r[...].astype(F32), axis=0).astype(BF16)
    small = jnp.sum(sm_r[...], axis=0)
    sm2_s[...] = small
    sm2_r[tm] = small
    gdec_out[...] = small[0:1]

    def rs_tm(p, slot):
        return tm_copy(
            quarter.at[pl.ds(p * pa, pa)], rs_t.at[slot], t_ss.at[0, p], t_rs.at[0, slot], p)

    def small_tm(p, slot):
        return tm_copy(sm2_s, sm2_r.at[slot], t_ss.at[1, p], t_rs.at[1, slot], p)

    others(n_tm, tm, lambda p: rs_tm(p, tm).start())
    others(n_tm, tm, lambda p: small_tm(p, tm).start())
    others(n_tm, tm, lambda p: rb_tm(p, p).wait_recv())
    eighth[...] = jnp.sum(rb_t[...].astype(F32), axis=0).astype(BF16)
    others(n_rows, row, lambda p: rb_row(p, row).start())
    rb_r[row] = eighth[pl.ds(row * pb, pb)]
    rs_t[tm] = quarter[pl.ds(tm * pa, pa)]
    others(n_tm, tm, lambda p: rs_tm(p, p).wait_recv())
    total = jnp.sum(rs_t[...].astype(F32), axis=0).astype(BF16)
    piece[...] = total
    full[row, tm] = total

    def ag_tm(p, slot):
        return tm_copy(piece, full.at[row, slot], gt_ss.at[p], gt_rs.at[slot], p)

    def ag_row(p, slot):
        return row_copy(full.at[row], full.at[slot], gr_ss.at[p], gr_rs.at[slot], p)

    others(n_tm, tm, lambda p: ag_tm(p, tm).start())
    others(n_rows, row, lambda p: rb_row(p, p).wait_recv())
    total_b = jnp.sum(rb_r[...].astype(F32), axis=0).astype(BF16)
    piece_b[...] = total_b
    full_b[tm, row] = total_b
    others(n_rows, row, lambda p: hb_row(p, row).start())
    others(n_tm, tm, lambda p: small_tm(p, p).wait_recv())
    ggain_out[...] = jnp.sum(sm2_r[...], axis=0)[1:2, 0:ch]
    others(n_tm, tm, lambda p: ag_tm(p, p).wait_recv())
    others(n_rows, row, lambda p: ag_row(p, row).start())
    others(n_rows, row, lambda p: hb_row(p, p).wait_recv())
    others(n_tm, tm, lambda p: hb_tm(p, tm).start())
    others(n_rows, row, lambda p: ag_row(p, p).wait_recv())

    def emit(source, low, high):
        half = section * 128 // s_ch
        cuts = [(0, section)] + [
            (section + h * half, section + (h + 1) * half) for h in range(s_ch // 128)]
        for which, (begin, end) in enumerate(cuts):
            a, b = max(begin, low), min(end, high)
            if a >= b:
                continue
            value = source[a - low : b - low].astype(F32).reshape((b - a) * 16, 128)
            rows = slice((a - begin) * 16, (b - begin) * 16)
            if which == 0:
                gout_out[rows, :] = value
            else:
                gin_out[rows, (which - 1) * 128 : which * 128] = value

    emit(full[...].reshape(na, 16, 128), 0, na)
    others(n_tm, tm, lambda p: hb_tm(p, p).wait_recv())
    emit(full_b[...].reshape(n_tm * qb, 16, 128), na, na + n_tm * qb)

    halo_end(halo_s, halo_r, halo_ss, halo_rs)
    halo_end(halo2_s, halo2_r, halo2_ss, halo2_rs)

    if groups > 1:
        @pl.when(has_after)
        def _():
            carry_f().wait_send()

        @pl.when(has_before)
        def _():
            carry_b().wait_send()

    def g_sends(p):
        g_copy(dec_s, dec_all.at[me], dec_ss.at[p], dec_rs.at[me], p).wait_send()
        g_copy(st_d.at[p], rc_d.at[me], a_ss.at[0, p], a_rs.at[0, me], p).wait_send()
        g_copy(st_o.at[p], rc_o.at[me], a_ss.at[1, p], a_rs.at[1, me], p).wait_send()
        g_copy(out_s.at[p], got_s.at[me], b_ss.at[0, p], b_rs.at[0, me], p).wait_send()
        g_copy(out_j.at[p], got_j.at[me], b_ss.at[1, p], b_rs.at[1, me], p).wait_send()
        g_copy(dp_s.at[p], dp_r.at[me], b_ss.at[2, p], b_rs.at[2, me], p).wait_send()

    def tm_sends(p):
        rs_tm(p, tm).wait_send()
        small_tm(p, tm).wait_send()
        ag_tm(p, tm).wait_send()
        rb_tm(p, tm).wait_send()
        hb_tm(p, tm).wait_send()

    def row_sends(p):
        rs_row(p, row).wait_send()
        small_row(p, row).wait_send()
        ag_row(p, row).wait_send()
        rb_row(p, row).wait_send()
        hb_row(p, row).wait_send()

    others(g, me, g_sends)
    others(n_tm, tm, tm_sends)
    others(n_rows, row, row_sends)


def write_out(*refs):
    sem = refs[12]
    copies = [pltpu.make_async_copy(refs[i], refs[6 + i], sem.at[i]) for i in range(6)]
    for copy in copies:
        copy.start()
    for copy in copies:
        copy.wait()


def on_device(n_tm, n_rows, frames, decays, in_weight, out_weight, skip_gain, cotangent):
    frame_count, band, across, ch = frames.shape
    s_ch = in_weight.shape[3]
    cells = band * across
    assert frame_count == 1 and n_tm % 4 == 0 and cells % 32 == 0
    assert ch == 128 and s_ch % 128 == 0 and across % 16 == 0
    cell_norm = 1.0 / math.sqrt(frame_count * n_tm * band * n_rows * across)
    frame_norm = 1.0 / math.sqrt(band * n_rows * across)
    g = 4
    chunk = cells // g
    devices = n_tm * n_rows
    used = 18 * ch * s_ch // 2048
    pa = -(-2 * used // (3 * devices))
    pb = max(1, -(-(used - pa * devices) // devices))
    vmem = pltpu.VMEM
    parts = lambda kind: vmem((g, chunk, s_ch), kind)
    dma = pltpu.SemaphoreType.DMA
    scratch = [
        vmem((2, 2, across, ch), BF16), vmem((2, 2, across, ch), BF16),
        vmem((8, s_ch), F32), vmem((g, 8, s_ch), F32),
        vmem((band + 2, across, 3 * ch), BF16), vmem((band + 2, across, 3 * ch), BF16),
        parts(BF16), parts(BF16), parts(BF16), parts(BF16),
        vmem((g + 1, chunk, s_ch), F32), parts(F32),
        parts(BF16), parts(BF16),
        vmem((g, 8, s_ch), F32), vmem((g, 8, s_ch), F32),
        parts(BF16), parts(BF16),
        vmem((chunk, s_ch), BF16), vmem((chunk, s_ch), BF16),
        vmem((chunk, s_ch), BF16), vmem((chunk, s_ch), BF16),
        vmem((2, 2, across, s_ch), BF16), vmem((2, 2, across, s_ch), BF16),
        vmem((band + 2, across, 3 * s_ch), BF16), vmem((band + 2, across, 3 * s_ch), BF16),
        vmem((devices * (pa + pb), 16, 128), BF16),
        vmem((n_rows, n_tm * pa, 16, 128), BF16),
        vmem((n_tm * pa, 16, 128), BF16),
        vmem((n_tm, pa, 16, 128), BF16),
        vmem((pa, 16, 128), BF16),
        vmem((n_rows, n_tm, pa, 16, 128), BF16),
        vmem((n_tm, n_rows * pb, 16, 128), BF16),
        vmem((n_rows * pb, 16, 128), BF16),
        vmem((n_rows, pb, 16, 128), BF16),
        vmem((pb, 16, 128), BF16),
        vmem((n_tm, n_rows, pb, 16, 128), BF16),
        vmem((8, s_ch), F32), vmem((n_rows, 8, s_ch), F32),
        vmem((8, s_ch), F32), vmem((n_tm, 8, s_ch), F32),
        dma((2,)), dma((2,)), dma((2,)), dma((2,)), dma((g,)), dma((g,)),
        dma((2, g)), dma((2, g)), dma((3, g)), dma((3, g)),
        dma((2, n_rows)), dma((2, n_rows)), dma((2, n_tm)), dma((2, n_tm)),
        dma((n_tm,)), dma((n_tm,)), dma((n_rows,)), dma((n_rows,)),
        dma((n_tm,)), dma((n_tm,)), dma((n_rows,)), dma((n_rows,)),
        dma((n_rows,)), dma((n_rows,)), dma((n_tm,)), dma((n_tm,)), dma((2,)), dma((2,)),
    ]
    results = pl.pallas_call(
        functools.partial(kernel, n_tm, n_rows, g, pa, pb, cell_norm, frame_norm),
        out_shape=(
            jax.ShapeDtypeStruct(frames.shape, BF16),
            jax.ShapeDtypeStruct(frames.shape, BF16),
            jax.ShapeDtypeStruct((9 * ch, s_ch), F32),
            jax.ShapeDtypeStruct((9 * s_ch, ch), F32),
            jax.ShapeDtypeStruct((1, ch), F32),
            jax.ShapeDtypeStruct((1, s_ch), F32),
        ),
        in_specs=[pl.BlockSpec(memory_space=pltpu.VMEM)] * 6,
        out_specs=[pl.BlockSpec(memory_space=pltpu.VMEM)] * 6,
        scratch_shapes=scratch,
        compiler_params=pltpu.CompilerParams(
            collective_id=0, has_side_effects=True, vmem_limit_bytes=48 * 2**20),
    )(frames, decays, in_weight, out_weight, skip_gain.reshape(1, ch), cotangent)
    y, dx, gin, gout, ggain, gdec = pl.pallas_call(
        write_out,
        out_shape=tuple(jax.ShapeDtypeStruct(a.shape, a.dtype) for a in results),
        in_specs=[pl.BlockSpec(memory_space=pltpu.VMEM)] * 6,
        out_specs=[pl.BlockSpec(memory_space=pl.ANY)] * 6,
        scratch_shapes=[dma((6,))],
        compiler_params=pltpu.CompilerParams(vmem_limit_bytes=2**20),
    )(*results)
    return (y, dx, gin.reshape(3, 3, ch, s_ch), gout.reshape(3, 3, s_ch, ch),
            ggain.reshape(ch), gdec)


def solution(mesh):
    in_specs = (
        P("tm", "rows", None, None),
        P("tm", None),
        P(),
        P(),
        P(),
        P("tm", "rows", None, None),
    )
    out_specs = (
        P("tm", "rows", None, None),
        P("tm", "rows", None, None),
        P(),
        P(),
        P(),
        P("tm", None),
    )
    body = functools.partial(on_device, mesh.shape["tm"], mesh.shape["rows"])
    return jax.shard_map(
        body, mesh=mesh, in_specs=in_specs, out_specs=out_specs, check_vma=False
    )
```

```python
import functools
import math

import jax
import jax.numpy as jnp
from jax import lax
from jax.experimental import pallas as pl
from jax.experimental.pallas import tpu as pltpu
from jax.sharding import PartitionSpec as P

F32 = jnp.float32
BF16 = jnp.bfloat16
MESH = pl.DeviceIdType.MESH


def dot_nn(a, b):
    return lax.dot_general(a, b, (((1,), (0,)), ((), ())), preferred_element_type=F32)


def dot_nt(a, b):
    return lax.dot_general(a, b, (((1,), (1,)), ((), ())), preferred_element_type=F32)


def dot_tn(a, b):
    return lax.dot_general(a, b, (((0,), (0,)), ((), ())), preferred_element_type=F32)


def put_shifted(cat, first, value, across):
    cells, width = value.shape
    rows = cells // across
    wide = value.astype(F32)
    column = lax.broadcasted_iota(jnp.int32, (rows, across, width), 1)
    left = pltpu.roll(wide, 1, 0).reshape(rows, across, width)
    right = pltpu.roll(wide, cells - 1, 0).reshape(rows, across, width)
    cat[first : first + rows, :, 0:width] = jnp.where(column == 0, 0.0, left).astype(BF16)
    cat[first : first + rows, :, width : 2 * width] = value.reshape(rows, across, width)
    cat[first : first + rows, :, 2 * width : 3 * width] = jnp.where(
        column == across - 1, 0.0, right
    ).astype(BF16)


def kernel(
    n_tm, n_rows, g, pa, pb, cell_norm, frame_norm,
    frames, decays, in_w, out_w, gain, cot,
    y_out, dx_out, gin_out, gout_out, ggain_out, gdec_out,
    halo_s, halo_r, dec_s, dec_all, cat_f, cat_c,
    st_d, st_o, rc_d, rc_o, st32, ad32, out_s, out_j, dp_s, dp_r, got_s, got_j,
    cf_s, cf_r, cb_s, cb_r,
    halo2_s, halo2_r, cat_s, cat_j,
    grads, rs_r, quarter, rs_t, piece, full,
    rb_t, eighth, rb_r, piece_b, full_b, sm_s, sm_r, sm2_s, sm2_r,
    halo_ss, halo_rs, halo2_ss, halo2_rs, dec_ss, dec_rs,
    a_ss, a_rs, b_ss, b_rs, r_ss, r_rs, t_ss, t_rs, gt_ss, gt_rs, gr_ss, gr_rs,
    bt_ss, bt_rs, br_ss, br_rs, hr_ss, hr_rs, ht_ss, ht_rs, c_ss, c_rs,
):
    tm = lax.axis_index("tm")
    row = lax.axis_index("rows")
    _, band, across, ch = frames.shape
    s_ch = in_w.shape[3]
    cells = band * across
    chunk = cells // g
    qa = n_tm * pa
    qb = n_rows * pb
    na = n_rows * qa
    groups = n_tm // g
    group = tm // g
    me = lax.rem(tm, g)
    first = group * g

    def flat(ref):
        if chunk % 16 == 0:
            return ref[...].reshape(cells, s_ch)
        return ref[...].astype(F32).reshape(cells, s_ch).astype(BF16)

    def others(axis_n, me, body):
        def one(s, carry):
            body(lax.rem(me + s, axis_n))
            return carry

        lax.fori_loop(1, axis_n, one, 0)

    def tm_copy(src, dst, ss, rs, peer):
        return pltpu.make_async_remote_copy(
            src_ref=src, dst_ref=dst, send_sem=ss, recv_sem=rs,
            device_id={"tm": peer}, device_id_type=MESH,
        )

    def g_copy(src, dst, ss, rs, peer):
        return tm_copy(src, dst, ss, rs, first + peer)

    def row_copy(src, dst, ss, rs, peer):
        return pltpu.make_async_remote_copy(
            src_ref=src, dst_ref=dst, send_sem=ss, recv_sem=rs,
            device_id={"rows": peer}, device_id_type=MESH,
        )

    has_low = row > 0
    has_high = row < n_rows - 1

    def halo_up(s, r, ss, rs):
        return row_copy(s.at[0], r.at[1], ss.at[0], rs.at[1], row - 1)

    def halo_down(s, r, ss, rs):
        return row_copy(s.at[1], r.at[0], ss.at[1], rs.at[0], row + 1)

    def halo_start(s, r, ss, rs):
        @pl.when(has_low)
        def _():
            halo_up(s, r, ss, rs).start()

        @pl.when(has_high)
        def _():
            halo_down(s, r, ss, rs).start()

        @pl.when(jnp.logical_not(has_low))
        def _():
            r[0] = jnp.zeros(r.shape[1:], r.dtype)

        @pl.when(jnp.logical_not(has_high))
        def _():
            r[1] = jnp.zeros(r.shape[1:], r.dtype)

    def halo_wait(s, r, ss, rs):
        @pl.when(has_low)
        def _():
            row_copy(s.at[0], r.at[0], ss.at[0], rs.at[0], row - 1).wait_recv()

        @pl.when(has_high)
        def _():
            row_copy(s.at[1], r.at[1], ss.at[1], rs.at[1], row + 1).wait_recv()

    def halo_end(s, r, ss, rs):
        @pl.when(has_low)
        def _():
            halo_up(s, r, ss, rs).wait_send()

        @pl.when(has_high)
        def _():
            halo_down(s, r, ss, rs).wait_send()

    barrier = pltpu.get_barrier_semaphore()
    others(n_tm, tm, lambda p: pl.semaphore_signal(
        barrier, inc=1, device_id={"tm": p}, device_id_type=MESH))
    others(n_rows, row, lambda p: pl.semaphore_signal(
        barrier, inc=1, device_id={"rows": p}, device_id_type=MESH))
    halo_s[0, 0] = frames[0, 0]
    halo_s[0, 1] = cot[0, 0]
    halo_s[1, 0] = frames[0, band - 1]
    halo_s[1, 1] = cot[0, band - 1]
    own_decay = jnp.broadcast_to(decays[...], (8, s_ch))
    dec_s[...] = own_decay
    dec_all[me] = own_decay
    pl.semaphore_wait(barrier, n_tm - 1 + n_rows - 1)

    halo_start(halo_s, halo_r, halo_ss, halo_rs)
    others(g, me, lambda p: g_copy(
        dec_s, dec_all.at[me], dec_ss.at[p], dec_rs.at[me], p).start())

    frames_own = frames[0].reshape(cells, ch)
    cot_own = cot[0].reshape(cells, ch)
    put_shifted(cat_f, 1, frames_own, across)
    put_shifted(cat_c, 1, cot_own, across)
    gain_sum = jnp.sum(
        frames_own.astype(F32) * cot_own.astype(F32), axis=0, keepdims=True) * cell_norm
    sm_s[...] = jnp.zeros(sm_s.shape, F32)
    sm_s[1:2, 0:ch] = gain_sum

    halo_wait(halo_s, halo_r, halo_ss, halo_rs)
    put_shifted(cat_f, 0, halo_r[0, 0], across)
    put_shifted(cat_f, band + 1, halo_r[1, 0], across)
    put_shifted(cat_c, 0, halo_r[0, 1], across)
    put_shifted(cat_c, band + 1, halo_r[1, 1], across)

    acc = None
    for i in range(3):
        term = dot_nn(cat_f[i : i + band].reshape(cells, 3 * ch), in_w[i].reshape(3 * ch, s_ch))
        acc = term if acc is None else acc + term
    st_d[...] = acc.reshape(g, chunk, s_ch).astype(BF16)
    others(g, me, lambda p: g_copy(
        st_d.at[p], rc_d.at[me], a_ss.at[0, p], a_rs.at[0, me], p).start())
    rc_d[me] = st_d[me]

    acc = None
    for i in range(3):
        for j in range(3):
            window = cat_c[i : i + band, :, j * ch : (j + 1) * ch].reshape(cells, ch)
            term = dot_nt(window, out_w[2 - i, 2 - j])
            acc = term if acc is None else acc + term
    st_o[...] = acc.reshape(g, chunk, s_ch).astype(BF16)
    others(g, me, lambda p: g_copy(
        st_o.at[p], rc_o.at[me], a_ss.at[1, p], a_rs.at[1, me], p).start())
    rc_o[me] = st_o[me]

    others(g, me, lambda p: g_copy(
        dec_s, dec_all.at[p], dec_ss.at[p], dec_rs.at[p], p).wait_recv())
    others(g, me, lambda p: g_copy(
        st_d.at[p], rc_d.at[p], a_ss.at[0, p], a_rs.at[0, p], p).wait_recv())
    zero = jnp.zeros((chunk, s_ch), F32)

    def carry_f():
        return tm_copy(cf_s, cf_r, c_ss.at[0], c_rs.at[0], tm + g)

    def carry_b():
        return tm_copy(cb_s, cb_r, c_ss.at[1], c_rs.at[1], tm - g)

    has_before = group > 0
    has_after = group < groups - 1

    def forward(t, state):
        state = dec_all[t][0:1] * state + rc_d[t].astype(F32)
        st32[t + 1] = state
        return state

    state_end = lax.fori_loop(0, g, forward, zero)

    @pl.when(jnp.logical_not(has_before))
    def _():
        cf_r[...] = jnp.zeros(cf_r.shape, BF16)
        if groups > 1:
            cf_s[...] = state_end.astype(BF16)
            carry_f().start()

    others(g, me, lambda p: g_copy(
        st_o.at[p], rc_o.at[p], a_ss.at[1, p], a_rs.at[1, p], p).wait_recv())

    def backward(turn, carried):
        t = g - 1 - turn
        adjoint = rc_o[t].astype(F32) + carried
        ad32[t] = adjoint
        return dec_all[t][0:1] * adjoint

    adjoint_end = lax.fori_loop(0, g, backward, zero)

    @pl.when(jnp.logical_not(has_after))
    def _():
        cb_r[...] = jnp.zeros(cb_r.shape, BF16)
        if groups > 1:
            cb_s[...] = adjoint_end.astype(BF16)
            carry_b().start()

    decay_all = dec_all[0][0:1]
    for t in range(1, g):
        decay_all = decay_all * dec_all[t][0:1]

    @pl.when(has_before)
    def _():
        tm_copy(cf_s, cf_r, c_ss.at[0], c_rs.at[0], tm - g).wait_recv()

        @pl.when(has_after)
        def _():
            cf_s[...] = (st32[g] + decay_all * cf_r[...].astype(F32)).astype(BF16)
            carry_f().start()

    def forward_fix(t, carried):
        carried = dec_all[t][0:1] * carried
        state = st32[t + 1] + carried
        st32[t + 1] = state
        out_s[t] = state.astype(BF16)
        return carried

    state_in = cf_r[...].astype(F32)
    st32[0] = state_in
    lax.fori_loop(0, g, forward_fix, state_in)
    others(g, me, lambda p: g_copy(
        out_s.at[p], got_s.at[me], b_ss.at[0, p], b_rs.at[0, me], p).start())
    got_s[me] = out_s[me]

    @pl.when(has_after)
    def _():
        tm_copy(cb_s, cb_r, c_ss.at[1], c_rs.at[1], tm + g).wait_recv()

        @pl.when(has_before)
        def _():
            cb_s[...] = (
                dec_all[0][0:1] * ad32[0] + decay_all * cb_r[...].astype(F32)).astype(BF16)
            carry_b().start()

    def backward_fix(turn, carried):
        t = g - 1 - turn
        adjoint = ad32[t] + carried
        out_j[t] = adjoint.astype(BF16)
        dp_s[t] = jnp.sum((adjoint * st32[t]).reshape(chunk // 8, 8, s_ch), axis=0)
        return dec_all[t][0:1] * carried

    lax.fori_loop(0, g, backward_fix, cb_r[...].astype(F32))
    others(g, me, lambda p: g_copy(
        out_j.at[p], got_j.at[me], b_ss.at[1, p], b_rs.at[1, me], p).start())
    others(g, me, lambda p: g_copy(
        dp_s.at[p], dp_r.at[me], b_ss.at[2, p], b_rs.at[2, me], p).start())
    got_j[me] = out_j[me]
    dp_r[me] = dp_s[me]

    def rs_row(p, slot):
        return row_copy(
            grads.at[pl.ds(p * qa, qa)], rs_r.at[slot], r_ss.at[0, p], r_rs.at[0, slot], p)

    def small_row(p, slot):
        return row_copy(sm_s, sm_r.at[slot], r_ss.at[1, p], r_rs.at[1, slot], p)

    def rb_tm(p, slot):
        return tm_copy(
            grads.at[pl.ds(na + p * qb, qb)], rb_t.at[slot], bt_ss.at[p], bt_rs.at[slot], p)

    def rb_row(p, slot):
        return row_copy(
            eighth.at[pl.ds(p * pb, pb)], rb_r.at[slot], br_ss.at[p], br_rs.at[slot], p)

    def hb_row(p, slot):
        return row_copy(piece_b, full_b.at[tm, slot], hr_ss.at[p], hr_rs.at[slot], p)

    def hb_tm(p, slot):
        return tm_copy(full_b.at[tm], full_b.at[slot], ht_ss.at[p], ht_rs.at[slot], p)

    section = 9 * s_ch * ch // 2048
    early = section // qa

    def rs_early(p):
        @pl.when(p < early)
        def _():
            rs_row(p, row).start()

    def rs_late(p):
        @pl.when(p >= early)
        def _():
            rs_row(p, row).start()

    others(g, me, lambda p: g_copy(
        out_s.at[p], got_s.at[p], b_ss.at[0, p], b_rs.at[0, p], p).wait_recv())
    states_own = flat(got_s)
    for i in range(3):
        value = dot_tn(states_own, cat_c[i : i + band].reshape(cells, 3 * ch)) * cell_norm
        for j in range(3):
            tap = (2 - i) * 3 + 2 - j
            base = tap * (s_ch // 16)
            grads[base : base + s_ch // 16] = (
                value[:, j * ch : (j + 1) * ch].astype(BF16).reshape(s_ch // 16, 16, ch))
    others(n_rows, row, rs_early)

    others(g, me, lambda p: g_copy(
        out_j.at[p], got_j.at[p], b_ss.at[1, p], b_rs.at[1, p], p).wait_recv())
    adj_own = flat(got_j)
    halo2_s[0, 0] = states_own[0:across]
    halo2_s[0, 1] = adj_own[0:across]
    halo2_s[1, 0] = states_own[cells - across :]
    halo2_s[1, 1] = adj_own[cells - across :]
    halo_start(halo2_s, halo2_r, halo2_ss, halo2_rs)
    blocks = 3 * ch // 16
    for i in range(3):
        value = dot_tn(cat_f[i : i + band].reshape(cells, 3 * ch), adj_own) * cell_norm
        for h in range(s_ch // 128):
            base = section + (h * 3 + i) * blocks
            grads[base : base + blocks] = (
                value[:, h * 128 : (h + 1) * 128].astype(BF16).reshape(blocks, 16, 128))
    if 2 * section < na + n_tm * qb:
        grads[2 * section :] = jnp.zeros((na + n_tm * qb - 2 * section, 16, 128), BF16)
    others(n_rows, row, rs_late)
    others(n_tm, tm, lambda p: rb_tm(p, tm).start())
    rs_r[row] = grads[pl.ds(row * qa, qa)]
    rb_t[tm] = grads[pl.ds(na + tm * qb, qb)]
    others(g, me, lambda p: g_copy(
        dp_s.at[p], dp_r.at[p], b_ss.at[2, p], b_rs.at[2, p], p).wait_recv())
    sm_s[0:1] = jnp.sum(jnp.sum(dp_r[...], axis=0), axis=0, keepdims=True) * frame_norm
    sm_r[row] = sm_s[...]
    others(n_rows, row, lambda p: small_row(p, row).start())

    halo_wait(halo2_s, halo2_r, halo2_ss, halo2_rs)
    put_shifted(cat_s, 0, halo2_r[0, 0], across)
    put_shifted(cat_s, 1, states_own, across)
    put_shifted(cat_s, band + 1, halo2_r[1, 0], across)
    put_shifted(cat_j, 0, halo2_r[0, 1], across)
    put_shifted(cat_j, 1, adj_own, across)
    put_shifted(cat_j, band + 1, halo2_r[1, 1], across)
    acc = gain[...] * frames_own.astype(F32)
    for i in range(3):
        acc = acc + dot_nn(
            cat_s[i : i + band].reshape(cells, 3 * s_ch), out_w[i].reshape(3 * s_ch, ch))
    y_out[0] = acc.astype(BF16).reshape(band, across, ch)
    acc = gain[...] * cot_own.astype(F32)
    for i in range(3):
        for j in range(3):
            window = cat_j[i : i + band, :, j * s_ch : (j + 1) * s_ch].reshape(cells, s_ch)
            acc = acc + dot_nt(window, in_w[2 - i, 2 - j])
    dx_out[0] = acc.astype(BF16).reshape(band, across, ch)

    others(n_rows, row, lambda p: rs_row(p, p).wait_recv())
    others(n_rows, row, lambda p: small_row(p, p).wait_recv())
    quarter[...] = jnp.sum(rs_r[...].astype(F32), axis=0).astype(BF16)
    small = jnp.sum(sm_r[...], axis=0)
    sm2_s[...] = small
    sm2_r[tm] = small
    gdec_out[...] = small[0:1]

    def rs_tm(p, slot):
        return tm_copy(
            quarter.at[pl.ds(p * pa, pa)], rs_t.at[slot], t_ss.at[0, p], t_rs.at[0, slot], p)

    def small_tm(p, slot):
        return tm_copy(sm2_s, sm2_r.at[slot], t_ss.at[1, p], t_rs.at[1, slot], p)

    others(n_tm, tm, lambda p: rs_tm(p, tm).start())
    others(n_tm, tm, lambda p: small_tm(p, tm).start())
    others(n_tm, tm, lambda p: rb_tm(p, p).wait_recv())
    eighth[...] = jnp.sum(rb_t[...].astype(F32), axis=0).astype(BF16)
    others(n_rows, row, lambda p: rb_row(p, row).start())
    rb_r[row] = eighth[pl.ds(row * pb, pb)]
    rs_t[tm] = quarter[pl.ds(tm * pa, pa)]
    others(n_tm, tm, lambda p: rs_tm(p, p).wait_recv())
    total = jnp.sum(rs_t[...].astype(F32), axis=0).astype(BF16)
    piece[...] = total
    full[row, tm] = total

    def ag_tm(p, slot):
        return tm_copy(piece, full.at[row, slot], gt_ss.at[p], gt_rs.at[slot], p)

    def ag_row(q, p, slot):
        return row_copy(
            full.at[row, q], full.at[slot, q], gr_ss.at[q, p], gr_rs.at[q, slot], p)

    def forward_piece(q):
        others(n_rows, row, lambda p: ag_row(q, p, row).start())

    others(n_tm, tm, lambda p: ag_tm(p, tm).start())
    forward_piece(tm)
    others(n_rows, row, lambda p: rb_row(p, p).wait_recv())
    total_b = jnp.sum(rb_r[...].astype(F32), axis=0).astype(BF16)
    piece_b[...] = total_b
    full_b[tm, row] = total_b
    others(n_rows, row, lambda p: hb_row(p, row).start())
    others(n_tm, tm, lambda p: small_tm(p, p).wait_recv())
    ggain_out[...] = jnp.sum(sm2_r[...], axis=0)[1:2, 0:ch]
    others(n_rows, row, lambda p: hb_row(p, p).wait_recv())
    others(n_tm, tm, lambda p: hb_tm(p, tm).start())

    def pass_on(q):
        ag_tm(q, q).wait_recv()
        forward_piece(q)

    others(n_tm, tm, pass_on)

    def piece_wait(q, carry):
        others(n_rows, row, lambda p: ag_row(q, p, p).wait_recv())
        return carry

    lax.fori_loop(0, n_tm, piece_wait, 0)

    def emit(source, low, high):
        half = section * 128 // s_ch
        cuts = [(0, section)] + [
            (section + h * half, section + (h + 1) * half) for h in range(s_ch // 128)]
        for which, (begin, end) in enumerate(cuts):
            a, b = max(begin, low), min(end, high)
            if a >= b:
                continue
            value = source[a - low : b - low].astype(F32).reshape((b - a) * 16, 128)
            rows = slice((a - begin) * 16, (b - begin) * 16)
            if which == 0:
                gout_out[rows, :] = value
            else:
                gin_out[rows, (which - 1) * 128 : which * 128] = value

    emit(full[...].reshape(na, 16, 128), 0, na)
    others(n_tm, tm, lambda p: hb_tm(p, p).wait_recv())
    emit(full_b[...].reshape(n_tm * qb, 16, 128), na, na + n_tm * qb)

    halo_end(halo_s, halo_r, halo_ss, halo_rs)
    halo_end(halo2_s, halo2_r, halo2_ss, halo2_rs)

    if groups > 1:
        @pl.when(has_after)
        def _():
            carry_f().wait_send()

        @pl.when(has_before)
        def _():
            carry_b().wait_send()

    def g_sends(p):
        g_copy(dec_s, dec_all.at[me], dec_ss.at[p], dec_rs.at[me], p).wait_send()
        g_copy(st_d.at[p], rc_d.at[me], a_ss.at[0, p], a_rs.at[0, me], p).wait_send()
        g_copy(st_o.at[p], rc_o.at[me], a_ss.at[1, p], a_rs.at[1, me], p).wait_send()
        g_copy(out_s.at[p], got_s.at[me], b_ss.at[0, p], b_rs.at[0, me], p).wait_send()
        g_copy(out_j.at[p], got_j.at[me], b_ss.at[1, p], b_rs.at[1, me], p).wait_send()
        g_copy(dp_s.at[p], dp_r.at[me], b_ss.at[2, p], b_rs.at[2, me], p).wait_send()

    def tm_sends(p):
        rs_tm(p, tm).wait_send()
        small_tm(p, tm).wait_send()
        ag_tm(p, tm).wait_send()
        rb_tm(p, tm).wait_send()
        hb_tm(p, tm).wait_send()

    def row_sends(p):
        rs_row(p, row).wait_send()
        small_row(p, row).wait_send()
        rb_row(p, row).wait_send()
        hb_row(p, row).wait_send()

    others(g, me, g_sends)
    others(n_tm, tm, tm_sends)
    others(n_rows, row, row_sends)

    def piece_sends(q, carry):
        others(n_rows, row, lambda p: ag_row(q, p, row).wait_send())
        return carry

    lax.fori_loop(0, n_tm, piece_sends, 0)


def write_out(*refs):
    sem = refs[12]
    copies = [pltpu.make_async_copy(refs[i], refs[6 + i], sem.at[i]) for i in range(6)]
    for copy in copies:
        copy.start()
    for copy in copies:
        copy.wait()


def on_device(n_tm, n_rows, frames, decays, in_weight, out_weight, skip_gain, cotangent):
    frame_count, band, across, ch = frames.shape
    s_ch = in_weight.shape[3]
    cells = band * across
    assert frame_count == 1 and n_tm % 4 == 0 and cells % 32 == 0
    assert ch == 128 and s_ch % 128 == 0 and across % 16 == 0
    cell_norm = 1.0 / math.sqrt(frame_count * n_tm * band * n_rows * across)
    frame_norm = 1.0 / math.sqrt(band * n_rows * across)
    g = 4
    chunk = cells // g
    devices = n_tm * n_rows
    used = 18 * ch * s_ch // 2048
    pa = -(-2 * used // (3 * devices))
    pb = max(1, -(-(used - pa * devices) // devices))
    vmem = pltpu.VMEM
    parts = lambda kind: vmem((g, chunk, s_ch), kind)
    dma = pltpu.SemaphoreType.DMA
    scratch = [
        vmem((2, 2, across, ch), BF16), vmem((2, 2, across, ch), BF16),
        vmem((8, s_ch), F32), vmem((g, 8, s_ch), F32),
        vmem((band + 2, across, 3 * ch), BF16), vmem((band + 2, across, 3 * ch), BF16),
        parts(BF16), parts(BF16), parts(BF16), parts(BF16),
        vmem((g + 1, chunk, s_ch), F32), parts(F32),
        parts(BF16), parts(BF16),
        vmem((g, 8, s_ch), F32), vmem((g, 8, s_ch), F32),
        parts(BF16), parts(BF16),
        vmem((chunk, s_ch), BF16), vmem((chunk, s_ch), BF16),
        vmem((chunk, s_ch), BF16), vmem((chunk, s_ch), BF16),
        vmem((2, 2, across, s_ch), BF16), vmem((2, 2, across, s_ch), BF16),
        vmem((band + 2, across, 3 * s_ch), BF16), vmem((band + 2, across, 3 * s_ch), BF16),
        vmem((devices * (pa + pb), 16, 128), BF16),
        vmem((n_rows, n_tm * pa, 16, 128), BF16),
        vmem((n_tm * pa, 16, 128), BF16),
        vmem((n_tm, pa, 16, 128), BF16),
        vmem((pa, 16, 128), BF16),
        vmem((n_rows, n_tm, pa, 16, 128), BF16),
        vmem((n_tm, n_rows * pb, 16, 128), BF16),
        vmem((n_rows * pb, 16, 128), BF16),
        vmem((n_rows, pb, 16, 128), BF16),
        vmem((pb, 16, 128), BF16),
        vmem((n_tm, n_rows, pb, 16, 128), BF16),
        vmem((8, s_ch), F32), vmem((n_rows, 8, s_ch), F32),
        vmem((8, s_ch), F32), vmem((n_tm, 8, s_ch), F32),
        dma((2,)), dma((2,)), dma((2,)), dma((2,)), dma((g,)), dma((g,)),
        dma((2, g)), dma((2, g)), dma((3, g)), dma((3, g)),
        dma((2, n_rows)), dma((2, n_rows)), dma((2, n_tm)), dma((2, n_tm)),
        dma((n_tm,)), dma((n_tm,)), dma((n_tm, n_rows)), dma((n_tm, n_rows)),
        dma((n_tm,)), dma((n_tm,)), dma((n_rows,)), dma((n_rows,)),
        dma((n_rows,)), dma((n_rows,)), dma((n_tm,)), dma((n_tm,)), dma((2,)), dma((2,)),
    ]
    results = pl.pallas_call(
        functools.partial(kernel, n_tm, n_rows, g, pa, pb, cell_norm, frame_norm),
        out_shape=(
            jax.ShapeDtypeStruct(frames.shape, BF16),
            jax.ShapeDtypeStruct(frames.shape, BF16),
            jax.ShapeDtypeStruct((9 * ch, s_ch), F32),
            jax.ShapeDtypeStruct((9 * s_ch, ch), F32),
            jax.ShapeDtypeStruct((1, ch), F32),
            jax.ShapeDtypeStruct((1, s_ch), F32),
        ),
        in_specs=[pl.BlockSpec(memory_space=pltpu.VMEM)] * 6,
        out_specs=[pl.BlockSpec(memory_space=pltpu.VMEM)] * 6,
        scratch_shapes=scratch,
        compiler_params=pltpu.CompilerParams(
            collective_id=0, has_side_effects=True, vmem_limit_bytes=48 * 2**20),
    )(frames, decays, in_weight, out_weight, skip_gain.reshape(1, ch), cotangent)
    y, dx, gin, gout, ggain, gdec = pl.pallas_call(
        write_out,
        out_shape=tuple(jax.ShapeDtypeStruct(a.shape, a.dtype) for a in results),
        in_specs=[pl.BlockSpec(memory_space=pltpu.VMEM)] * 6,
        out_specs=[pl.BlockSpec(memory_space=pl.ANY)] * 6,
        scratch_shapes=[dma((6,))],
        compiler_params=pltpu.CompilerParams(vmem_limit_bytes=2**20),
    )(*results)
    return (y, dx, gin.reshape(3, 3, ch, s_ch), gout.reshape(3, 3, s_ch, ch),
            ggain.reshape(ch), gdec)


def solution(mesh):
    in_specs = (
        P("tm", "rows", None, None),
        P("tm", None),
        P(),
        P(),
        P(),
        P("tm", "rows", None, None),
    )
    out_specs = (
        P("tm", "rows", None, None),
        P("tm", "rows", None, None),
        P(),
        P(),
        P(),
        P("tm", None),
    )
    body = functools.partial(on_device, mesh.shape["tm"], mesh.shape["rows"])
    return jax.shard_map(
        body, mesh=mesh, in_specs=in_specs, out_specs=out_specs, check_vma=False
    )
```

```python
import functools
import math

import jax
import jax.numpy as jnp
from jax import lax
from jax.experimental import pallas as pl
from jax.experimental.pallas import tpu as pltpu
from jax.sharding import PartitionSpec as P

F32 = jnp.float32
BF16 = jnp.bfloat16
MESH = pl.DeviceIdType.MESH


def dot_nn(a, b):
    return lax.dot_general(a, b, (((1,), (0,)), ((), ())), preferred_element_type=F32)


def dot_nt(a, b):
    return lax.dot_general(a, b, (((1,), (1,)), ((), ())), preferred_element_type=F32)


def dot_tn(a, b):
    return lax.dot_general(a, b, (((0,), (0,)), ((), ())), preferred_element_type=F32)


def put_shifted(cat, first, value, across):
    cells, width = value.shape
    rows = cells // across
    wide = value.astype(F32)
    column = lax.broadcasted_iota(jnp.int32, (rows, across, width), 1)
    left = pltpu.roll(wide, 1, 0).reshape(rows, across, width)
    right = pltpu.roll(wide, cells - 1, 0).reshape(rows, across, width)
    cat[first : first + rows, :, 0:width] = jnp.where(column == 0, 0.0, left).astype(BF16)
    cat[first : first + rows, :, width : 2 * width] = value.reshape(rows, across, width)
    cat[first : first + rows, :, 2 * width : 3 * width] = jnp.where(
        column == across - 1, 0.0, right
    ).astype(BF16)


def kernel(
    n_tm, n_rows, g, pa, pb, cell_norm, frame_norm,
    frames, decays, in_w, out_w, gain, cot,
    y_out, dx_out, gin_out, gout_out, ggain_out, gdec_out,
    halo_s, halo_r, dec_s, dec_all, cat_f, cat_c,
    st_d, st_o, rc_d, rc_o, st32, ad32, out_s, out_j, dp_s, dp_r, got_s, got_j,
    cf_s, cf_r, cb_s, cb_r,
    halo2_s, halo2_r, cat_s, cat_j,
    grads, rs_r, quarter, rs_t, piece, full,
    rb_t, eighth, rb_r, piece_b, full_b, sm_s, sm_r, sm2_s, sm2_r,
    halo_ss, halo_rs, halo2_ss, halo2_rs, dec_ss, dec_rs,
    a_ss, a_rs, b_ss, b_rs, r_ss, r_rs, t_ss, t_rs, gt_ss, gt_rs, gr_ss, gr_rs,
    bt_ss, bt_rs, br_ss, br_rs, hr_ss, hr_rs, ht_ss, ht_rs, c_ss, c_rs,
):
    tm = lax.axis_index("tm")
    row = lax.axis_index("rows")
    _, band, across, ch = frames.shape
    s_ch = in_w.shape[3]
    cells = band * across
    chunk = cells // g
    qa = n_tm * pa
    qb = n_rows * pb
    na = n_rows * qa
    groups = n_tm // g
    group = tm // g
    me = lax.rem(tm, g)
    first = group * g

    def flat(ref):
        if chunk % 16 == 0:
            return ref[...].reshape(cells, s_ch)
        return ref[...].astype(F32).reshape(cells, s_ch).astype(BF16)

    def others(axis_n, me, body):
        def one(s, carry):
            body(lax.rem(me + s, axis_n))
            return carry

        lax.fori_loop(1, axis_n, one, 0)

    def tm_copy(src, dst, ss, rs, peer):
        return pltpu.make_async_remote_copy(
            src_ref=src, dst_ref=dst, send_sem=ss, recv_sem=rs,
            device_id={"tm": peer}, device_id_type=MESH,
        )

    def g_copy(src, dst, ss, rs, peer):
        return tm_copy(src, dst, ss, rs, first + peer)

    def row_copy(src, dst, ss, rs, peer):
        return pltpu.make_async_remote_copy(
            src_ref=src, dst_ref=dst, send_sem=ss, recv_sem=rs,
            device_id={"rows": peer}, device_id_type=MESH,
        )

    has_low = row > 0
    has_high = row < n_rows - 1

    def halo_up(s, r, ss, rs):
        return row_copy(s.at[0], r.at[1], ss.at[0], rs.at[1], row - 1)

    def halo_down(s, r, ss, rs):
        return row_copy(s.at[1], r.at[0], ss.at[1], rs.at[0], row + 1)

    def halo_start(s, r, ss, rs):
        @pl.when(has_low)
        def _():
            halo_up(s, r, ss, rs).start()

        @pl.when(has_high)
        def _():
            halo_down(s, r, ss, rs).start()

        @pl.when(jnp.logical_not(has_low))
        def _():
            r[0] = jnp.zeros(r.shape[1:], r.dtype)

        @pl.when(jnp.logical_not(has_high))
        def _():
            r[1] = jnp.zeros(r.shape[1:], r.dtype)

    def halo_wait(s, r, ss, rs):
        @pl.when(has_low)
        def _():
            row_copy(s.at[0], r.at[0], ss.at[0], rs.at[0], row - 1).wait_recv()

        @pl.when(has_high)
        def _():
            row_copy(s.at[1], r.at[1], ss.at[1], rs.at[1], row + 1).wait_recv()

    def halo_end(s, r, ss, rs):
        @pl.when(has_low)
        def _():
            halo_up(s, r, ss, rs).wait_send()

        @pl.when(has_high)
        def _():
            halo_down(s, r, ss, rs).wait_send()

    barrier = pltpu.get_barrier_semaphore()
    others(n_tm, tm, lambda p: pl.semaphore_signal(
        barrier, inc=1, device_id={"tm": p}, device_id_type=MESH))
    others(n_rows, row, lambda p: pl.semaphore_signal(
        barrier, inc=1, device_id={"rows": p}, device_id_type=MESH))
    halo_s[0, 0] = frames[0, 0]
    halo_s[0, 1] = cot[0, 0]
    halo_s[1, 0] = frames[0, band - 1]
    halo_s[1, 1] = cot[0, band - 1]
    own_decay = jnp.broadcast_to(decays[...], (8, s_ch))
    dec_s[...] = own_decay
    dec_all[me] = own_decay
    pl.semaphore_wait(barrier, n_tm - 1 + n_rows - 1)

    halo_start(halo_s, halo_r, halo_ss, halo_rs)
    others(g, me, lambda p: g_copy(
        dec_s, dec_all.at[me], dec_ss.at[p], dec_rs.at[me], p).start())

    frames_own = frames[0].reshape(cells, ch)
    cot_own = cot[0].reshape(cells, ch)
    put_shifted(cat_f, 1, frames_own, across)
    put_shifted(cat_c, 1, cot_own, across)
    gain_sum = jnp.sum(
        frames_own.astype(F32) * cot_own.astype(F32), axis=0, keepdims=True) * cell_norm
    sm_s[...] = jnp.zeros(sm_s.shape, F32)
    sm_s[1:2, 0:ch] = gain_sum

    halo_wait(halo_s, halo_r, halo_ss, halo_rs)
    put_shifted(cat_f, 0, halo_r[0, 0], across)
    put_shifted(cat_f, band + 1, halo_r[1, 0], across)
    put_shifted(cat_c, 0, halo_r[0, 1], across)
    put_shifted(cat_c, band + 1, halo_r[1, 1], across)

    acc = None
    for i in range(3):
        term = dot_nn(cat_f[i : i + band].reshape(cells, 3 * ch), in_w[i].reshape(3 * ch, s_ch))
        acc = term if acc is None else acc + term
    st_d[...] = acc.reshape(g, chunk, s_ch).astype(BF16)
    others(g, me, lambda p: g_copy(
        st_d.at[p], rc_d.at[me], a_ss.at[0, p], a_rs.at[0, me], p).start())
    rc_d[me] = st_d[me]

    acc = None
    for i in range(3):
        for j in range(3):
            window = cat_c[i : i + band, :, j * ch : (j + 1) * ch].reshape(cells, ch)
            term = dot_nt(window, out_w[2 - i, 2 - j])
            acc = term if acc is None else acc + term
    st_o[...] = acc.reshape(g, chunk, s_ch).astype(BF16)
    others(g, me, lambda p: g_copy(
        st_o.at[p], rc_o.at[me], a_ss.at[1, p], a_rs.at[1, me], p).start())
    rc_o[me] = st_o[me]

    others(g, me, lambda p: g_copy(
        dec_s, dec_all.at[p], dec_ss.at[p], dec_rs.at[p], p).wait_recv())
    others(g, me, lambda p: g_copy(
        st_d.at[p], rc_d.at[p], a_ss.at[0, p], a_rs.at[0, p], p).wait_recv())
    zero = jnp.zeros((chunk, s_ch), F32)

    def carry_f():
        return tm_copy(cf_s, cf_r, c_ss.at[0], c_rs.at[0], tm + g)

    def carry_b():
        return tm_copy(cb_s, cb_r, c_ss.at[1], c_rs.at[1], tm - g)

    has_before = group > 0
    has_after = group < groups - 1

    def forward(t, state):
        state = dec_all[t][0:1] * state + rc_d[t].astype(F32)
        st32[t + 1] = state
        return state

    state_end = lax.fori_loop(0, g, forward, zero)

    @pl.when(jnp.logical_not(has_before))
    def _():
        cf_r[...] = jnp.zeros(cf_r.shape, BF16)
        if groups > 1:
            cf_s[...] = state_end.astype(BF16)
            carry_f().start()

    others(g, me, lambda p: g_copy(
        st_o.at[p], rc_o.at[p], a_ss.at[1, p], a_rs.at[1, p], p).wait_recv())

    def backward(turn, carried):
        t = g - 1 - turn
        adjoint = rc_o[t].astype(F32) + carried
        ad32[t] = adjoint
        return dec_all[t][0:1] * adjoint

    adjoint_end = lax.fori_loop(0, g, backward, zero)

    @pl.when(jnp.logical_not(has_after))
    def _():
        cb_r[...] = jnp.zeros(cb_r.shape, BF16)
        if groups > 1:
            cb_s[...] = adjoint_end.astype(BF16)
            carry_b().start()

    decay_all = dec_all[0][0:1]
    for t in range(1, g):
        decay_all = decay_all * dec_all[t][0:1]

    @pl.when(has_before)
    def _():
        tm_copy(cf_s, cf_r, c_ss.at[0], c_rs.at[0], tm - g).wait_recv()

        @pl.when(has_after)
        def _():
            cf_s[...] = (st32[g] + decay_all * cf_r[...].astype(F32)).astype(BF16)
            carry_f().start()

    def forward_fix(t, carried):
        carried = dec_all[t][0:1] * carried
        state = st32[t + 1] + carried
        st32[t + 1] = state
        out_s[t] = state.astype(BF16)
        return carried

    state_in = cf_r[...].astype(F32)
    st32[0] = state_in
    lax.fori_loop(0, g, forward_fix, state_in)
    others(g, me, lambda p: g_copy(
        out_s.at[p], got_s.at[me], b_ss.at[0, p], b_rs.at[0, me], p).start())
    got_s[me] = out_s[me]

    @pl.when(has_after)
    def _():
        tm_copy(cb_s, cb_r, c_ss.at[1], c_rs.at[1], tm + g).wait_recv()

        @pl.when(has_before)
        def _():
            cb_s[...] = (
                dec_all[0][0:1] * ad32[0] + decay_all * cb_r[...].astype(F32)).astype(BF16)
            carry_b().start()

    def backward_fix(turn, carried):
        t = g - 1 - turn
        adjoint = ad32[t] + carried
        out_j[t] = adjoint.astype(BF16)
        dp_s[t] = jnp.sum((adjoint * st32[t]).reshape(chunk // 8, 8, s_ch), axis=0)
        return dec_all[t][0:1] * carried

    lax.fori_loop(0, g, backward_fix, cb_r[...].astype(F32))
    others(g, me, lambda p: g_copy(
        out_j.at[p], got_j.at[me], b_ss.at[1, p], b_rs.at[1, me], p).start())
    others(g, me, lambda p: g_copy(
        dp_s.at[p], dp_r.at[me], b_ss.at[2, p], b_rs.at[2, me], p).start())
    got_j[me] = out_j[me]
    dp_r[me] = dp_s[me]

    def rs_row(p, slot):
        return row_copy(
            grads.at[pl.ds(p * qa, qa)], rs_r.at[slot], r_ss.at[0, p], r_rs.at[0, slot], p)

    def small_row(p, slot):
        return row_copy(sm_s, sm_r.at[slot], r_ss.at[1, p], r_rs.at[1, slot], p)

    def rb_tm(p, slot):
        return tm_copy(
            grads.at[pl.ds(na + p * qb, qb)], rb_t.at[slot], bt_ss.at[p], bt_rs.at[slot], p)

    def rb_row(p, slot):
        return row_copy(
            eighth.at[pl.ds(p * pb, pb)], rb_r.at[slot], br_ss.at[p], br_rs.at[slot], p)

    def hb_row(p, slot):
        return row_copy(piece_b, full_b.at[tm, slot], hr_ss.at[p], hr_rs.at[slot], p)

    def hb_tm(p, slot):
        return tm_copy(full_b.at[tm], full_b.at[slot], ht_ss.at[p], ht_rs.at[slot], p)

    section = 9 * s_ch * ch // 2048
    early = section // qa

    def rs_early(p):
        @pl.when(p < early)
        def _():
            rs_row(p, row).start()

    def rs_late(p):
        @pl.when(p >= early)
        def _():
            rs_row(p, row).start()

    others(g, me, lambda p: g_copy(
        out_s.at[p], got_s.at[p], b_ss.at[0, p], b_rs.at[0, p], p).wait_recv())
    states_own = flat(got_s)
    for i in range(3):
        value = dot_tn(states_own, cat_c[i : i + band].reshape(cells, 3 * ch)) * cell_norm
        for j in range(3):
            tap = (2 - i) * 3 + 2 - j
            base = tap * (s_ch // 16)
            grads[base : base + s_ch // 16] = (
                value[:, j * ch : (j + 1) * ch].astype(BF16).reshape(s_ch // 16, 16, ch))
    others(n_rows, row, rs_early)

    others(g, me, lambda p: g_copy(
        out_j.at[p], got_j.at[p], b_ss.at[1, p], b_rs.at[1, p], p).wait_recv())
    adj_own = flat(got_j)
    halo2_s[0, 0] = states_own[0:across]
    halo2_s[0, 1] = adj_own[0:across]
    halo2_s[1, 0] = states_own[cells - across :]
    halo2_s[1, 1] = adj_own[cells - across :]
    halo_start(halo2_s, halo2_r, halo2_ss, halo2_rs)
    blocks = 3 * ch // 16
    for i in range(3):
        value = dot_tn(cat_f[i : i + band].reshape(cells, 3 * ch), adj_own) * cell_norm
        for h in range(s_ch // 128):
            base = section + (h * 3 + i) * blocks
            grads[base : base + blocks] = (
                value[:, h * 128 : (h + 1) * 128].astype(BF16).reshape(blocks, 16, 128))
    if 2 * section < na + n_tm * qb:
        grads[2 * section :] = jnp.zeros((na + n_tm * qb - 2 * section, 16, 128), BF16)
    others(n_rows, row, rs_late)
    others(n_tm, tm, lambda p: rb_tm(p, tm).start())
    rs_r[row] = grads[pl.ds(row * qa, qa)]
    rb_t[tm] = grads[pl.ds(na + tm * qb, qb)]
    others(g, me, lambda p: g_copy(
        dp_s.at[p], dp_r.at[p], b_ss.at[2, p], b_rs.at[2, p], p).wait_recv())
    sm_s[0:1] = jnp.sum(jnp.sum(dp_r[...], axis=0), axis=0, keepdims=True) * frame_norm
    sm_r[row] = sm_s[...]
    others(n_rows, row, lambda p: small_row(p, row).start())

    halo_wait(halo2_s, halo2_r, halo2_ss, halo2_rs)
    put_shifted(cat_s, 0, halo2_r[0, 0], across)
    put_shifted(cat_s, 1, states_own, across)
    put_shifted(cat_s, band + 1, halo2_r[1, 0], across)
    put_shifted(cat_j, 0, halo2_r[0, 1], across)
    put_shifted(cat_j, 1, adj_own, across)
    put_shifted(cat_j, band + 1, halo2_r[1, 1], across)
    acc = gain[...] * frames_own.astype(F32)
    for i in range(3):
        acc = acc + dot_nn(
            cat_s[i : i + band].reshape(cells, 3 * s_ch), out_w[i].reshape(3 * s_ch, ch))
    y_out[0] = acc.astype(BF16).reshape(band, across, ch)
    acc = gain[...] * cot_own.astype(F32)
    for i in range(3):
        for j in range(3):
            window = cat_j[i : i + band, :, j * s_ch : (j + 1) * s_ch].reshape(cells, s_ch)
            acc = acc + dot_nt(window, in_w[2 - i, 2 - j])
    dx_out[0] = acc.astype(BF16).reshape(band, across, ch)

    others(n_rows, row, lambda p: rs_row(p, p).wait_recv())
    others(n_rows, row, lambda p: small_row(p, p).wait_recv())
    quarter[...] = jnp.sum(rs_r[...].astype(F32), axis=0).astype(BF16)
    small = jnp.sum(sm_r[...], axis=0)
    sm2_s[...] = small
    sm2_r[tm] = small
    gdec_out[...] = small[0:1]

    def rs_tm(p, slot):
        return tm_copy(
            quarter.at[pl.ds(p * pa, pa)], rs_t.at[slot], t_ss.at[0, p], t_rs.at[0, slot], p)

    def small_tm(p, slot):
        return tm_copy(sm2_s, sm2_r.at[slot], t_ss.at[1, p], t_rs.at[1, slot], p)

    others(n_tm, tm, lambda p: rs_tm(p, tm).start())
    others(n_tm, tm, lambda p: small_tm(p, tm).start())
    others(n_tm, tm, lambda p: rb_tm(p, p).wait_recv())
    eighth[...] = jnp.sum(rb_t[...].astype(F32), axis=0).astype(BF16)
    others(n_rows, row, lambda p: rb_row(p, row).start())
    rb_r[row] = eighth[pl.ds(row * pb, pb)]
    rs_t[tm] = quarter[pl.ds(tm * pa, pa)]
    others(n_tm, tm, lambda p: rs_tm(p, p).wait_recv())
    total = jnp.sum(rs_t[...].astype(F32), axis=0).astype(BF16)
    piece[...] = total
    full[row, tm] = total

    def ag_tm(p, slot):
        return tm_copy(piece, full.at[row, slot], gt_ss.at[p], gt_rs.at[slot], p)

    def ag_row(q, p, slot):
        return row_copy(
            full.at[row, q], full.at[slot, q], gr_ss.at[q, p], gr_rs.at[q, slot], p)

    def forward_piece(q):
        others(n_rows, row, lambda p: ag_row(q, p, row).start())

    others(n_tm, tm, lambda p: ag_tm(p, tm).start())
    forward_piece(tm)
    others(n_rows, row, lambda p: rb_row(p, p).wait_recv())
    total_b = jnp.sum(rb_r[...].astype(F32), axis=0).astype(BF16)
    piece_b[...] = total_b
    full_b[tm, row] = total_b
    others(n_rows, row, lambda p: hb_row(p, row).start())
    others(n_tm, tm, lambda p: small_tm(p, p).wait_recv())
    ggain_out[...] = jnp.sum(sm2_r[...], axis=0)[1:2, 0:ch]
    others(n_rows, row, lambda p: hb_row(p, p).wait_recv())
    others(n_tm, tm, lambda p: hb_tm(p, tm).start())

    def pass_on(q):
        ag_tm(q, q).wait_recv()
        forward_piece(q)

    others(n_tm, tm, pass_on)

    def piece_wait(q, carry):
        others(n_rows, row, lambda p: ag_row(q, p, p).wait_recv())
        return carry

    lax.fori_loop(0, n_tm, piece_wait, 0)

    def emit(source, low, high):
        half = section * 128 // s_ch
        cuts = [(0, section)] + [
            (section + h * half, section + (h + 1) * half) for h in range(s_ch // 128)]
        for which, (begin, end) in enumerate(cuts):
            a, b = max(begin, low), min(end, high)
            if a >= b:
                continue
            value = source[a - low : b - low].astype(F32).reshape((b - a) * 16, 128)
            rows = slice((a - begin) * 16, (b - begin) * 16)
            if which == 0:
                gout_out[rows, :] = value
            else:
                gin_out[rows, (which - 1) * 128 : which * 128] = value

    emit(full[...].reshape(na, 16, 128), 0, na)
    others(n_tm, tm, lambda p: hb_tm(p, p).wait_recv())
    emit(full_b[...].reshape(n_tm * qb, 16, 128), na, na + n_tm * qb)

    halo_end(halo_s, halo_r, halo_ss, halo_rs)
    halo_end(halo2_s, halo2_r, halo2_ss, halo2_rs)

    if groups > 1:
        @pl.when(has_after)
        def _():
            carry_f().wait_send()

        @pl.when(has_before)
        def _():
            carry_b().wait_send()

    def g_sends(p):
        g_copy(dec_s, dec_all.at[me], dec_ss.at[p], dec_rs.at[me], p).wait_send()
        g_copy(st_d.at[p], rc_d.at[me], a_ss.at[0, p], a_rs.at[0, me], p).wait_send()
        g_copy(st_o.at[p], rc_o.at[me], a_ss.at[1, p], a_rs.at[1, me], p).wait_send()
        g_copy(out_s.at[p], got_s.at[me], b_ss.at[0, p], b_rs.at[0, me], p).wait_send()
        g_copy(out_j.at[p], got_j.at[me], b_ss.at[1, p], b_rs.at[1, me], p).wait_send()
        g_copy(dp_s.at[p], dp_r.at[me], b_ss.at[2, p], b_rs.at[2, me], p).wait_send()

    def tm_sends(p):
        rs_tm(p, tm).wait_send()
        small_tm(p, tm).wait_send()
        ag_tm(p, tm).wait_send()
        rb_tm(p, tm).wait_send()
        hb_tm(p, tm).wait_send()

    def row_sends(p):
        rs_row(p, row).wait_send()
        small_row(p, row).wait_send()
        rb_row(p, row).wait_send()
        hb_row(p, row).wait_send()

    others(g, me, g_sends)
    others(n_tm, tm, tm_sends)
    others(n_rows, row, row_sends)

    def piece_sends(q, carry):
        others(n_rows, row, lambda p: ag_row(q, p, row).wait_send())
        return carry

    lax.fori_loop(0, n_tm, piece_sends, 0)


def write_out(*refs):
    sem = refs[12]
    copies = [pltpu.make_async_copy(refs[i], refs[6 + i], sem.at[i]) for i in range(6)]
    for copy in copies:
        copy.start()
    for copy in copies:
        copy.wait()


def on_device(n_tm, n_rows, frames, decays, in_weight, out_weight, skip_gain, cotangent):
    frame_count, band, across, ch = frames.shape
    s_ch = in_weight.shape[3]
    cells = band * across
    assert frame_count == 1 and n_tm % 4 == 0 and cells % 32 == 0
    assert ch == 128 and s_ch % 128 == 0 and across % 16 == 0
    cell_norm = 1.0 / math.sqrt(frame_count * n_tm * band * n_rows * across)
    frame_norm = 1.0 / math.sqrt(band * n_rows * across)
    g = 4
    chunk = cells // g
    devices = n_tm * n_rows
    used = 18 * ch * s_ch // 2048
    pa = -(-7 * used // (9 * devices))
    pb = max(1, -(-(used - pa * devices) // devices))
    vmem = pltpu.VMEM
    parts = lambda kind: vmem((g, chunk, s_ch), kind)
    dma = pltpu.SemaphoreType.DMA
    scratch = [
        vmem((2, 2, across, ch), BF16), vmem((2, 2, across, ch), BF16),
        vmem((8, s_ch), F32), vmem((g, 8, s_ch), F32),
        vmem((band + 2, across, 3 * ch), BF16), vmem((band + 2, across, 3 * ch), BF16),
        parts(BF16), parts(BF16), parts(BF16), parts(BF16),
        vmem((g + 1, chunk, s_ch), F32), parts(F32),
        parts(BF16), parts(BF16),
        vmem((g, 8, s_ch), F32), vmem((g, 8, s_ch), F32),
        parts(BF16), parts(BF16),
        vmem((chunk, s_ch), BF16), vmem((chunk, s_ch), BF16),
        vmem((chunk, s_ch), BF16), vmem((chunk, s_ch), BF16),
        vmem((2, 2, across, s_ch), BF16), vmem((2, 2, across, s_ch), BF16),
        vmem((band + 2, across, 3 * s_ch), BF16), vmem((band + 2, across, 3 * s_ch), BF16),
        vmem((devices * (pa + pb), 16, 128), BF16),
        vmem((n_rows, n_tm * pa, 16, 128), BF16),
        vmem((n_tm * pa, 16, 128), BF16),
        vmem((n_tm, pa, 16, 128), BF16),
        vmem((pa, 16, 128), BF16),
        vmem((n_rows, n_tm, pa, 16, 128), BF16),
        vmem((n_tm, n_rows * pb, 16, 128), BF16),
        vmem((n_rows * pb, 16, 128), BF16),
        vmem((n_rows, pb, 16, 128), BF16),
        vmem((pb, 16, 128), BF16),
        vmem((n_tm, n_rows, pb, 16, 128), BF16),
        vmem((8, s_ch), F32), vmem((n_rows, 8, s_ch), F32),
        vmem((8, s_ch), F32), vmem((n_tm, 8, s_ch), F32),
        dma((2,)), dma((2,)), dma((2,)), dma((2,)), dma((g,)), dma((g,)),
        dma((2, g)), dma((2, g)), dma((3, g)), dma((3, g)),
        dma((2, n_rows)), dma((2, n_rows)), dma((2, n_tm)), dma((2, n_tm)),
        dma((n_tm,)), dma((n_tm,)), dma((n_tm, n_rows)), dma((n_tm, n_rows)),
        dma((n_tm,)), dma((n_tm,)), dma((n_rows,)), dma((n_rows,)),
        dma((n_rows,)), dma((n_rows,)), dma((n_tm,)), dma((n_tm,)), dma((2,)), dma((2,)),
    ]
    results = pl.pallas_call(
        functools.partial(kernel, n_tm, n_rows, g, pa, pb, cell_norm, frame_norm),
        out_shape=(
            jax.ShapeDtypeStruct(frames.shape, BF16),
            jax.ShapeDtypeStruct(frames.shape, BF16),
            jax.ShapeDtypeStruct((9 * ch, s_ch), F32),
            jax.ShapeDtypeStruct((9 * s_ch, ch), F32),
            jax.ShapeDtypeStruct((1, ch), F32),
            jax.ShapeDtypeStruct((1, s_ch), F32),
        ),
        in_specs=[pl.BlockSpec(memory_space=pltpu.VMEM)] * 6,
        out_specs=[pl.BlockSpec(memory_space=pltpu.VMEM)] * 6,
        scratch_shapes=scratch,
        compiler_params=pltpu.CompilerParams(
            collective_id=0, has_side_effects=True, vmem_limit_bytes=48 * 2**20),
    )(frames, decays, in_weight, out_weight, skip_gain.reshape(1, ch), cotangent)
    y, dx, gin, gout, ggain, gdec = pl.pallas_call(
        write_out,
        out_shape=tuple(jax.ShapeDtypeStruct(a.shape, a.dtype) for a in results),
        in_specs=[pl.BlockSpec(memory_space=pltpu.VMEM)] * 6,
        out_specs=[pl.BlockSpec(memory_space=pl.ANY)] * 6,
        scratch_shapes=[dma((6,))],
        compiler_params=pltpu.CompilerParams(vmem_limit_bytes=2**20),
    )(*results)
    return (y, dx, gin.reshape(3, 3, ch, s_ch), gout.reshape(3, 3, s_ch, ch),
            ggain.reshape(ch), gdec)


def solution(mesh):
    in_specs = (
        P("tm", "rows", None, None),
        P("tm", None),
        P(),
        P(),
        P(),
        P("tm", "rows", None, None),
    )
    out_specs = (
        P("tm", "rows", None, None),
        P("tm", "rows", None, None),
        P(),
        P(),
        P(),
        P("tm", None),
    )
    body = functools.partial(on_device, mesh.shape["tm"], mesh.shape["rows"])
    return jax.shard_map(
        body, mesh=mesh, in_specs=in_specs, out_specs=out_specs, check_vma=False
    )
```
